512 devices in a mesh: panel: 2 (over y_lo), lon: 16 (over z, core), lat: 16 (over y_hi, x).
Axes of the slice: x: 4, y: 8 (y_hi: 4, y_lo: 2; y = y_hi * 2 + y_lo), z: 8, core: 2. Of those that a mesh axis runs over, the one named last changes fastest.
Arguments:
- pressure: float32 [2, 256, 512, 128], P('panel', 'lat', 'lon'), may hold values from -6 to 6
- porosity: float32 [2, 256, 512, 128], P('panel', 'lat', 'lon'), may hold values from 0.5 to 2
- source: float32 [2, 256, 512, 128], P('panel', 'lat', 'lon'), may hold values from -6 to 6
- bulk: float32 [2, 256, 512, 128], P('panel', 'lat', 'lon'), may hold values from 0.5 to 2
- lat_codes: int32 [2, 2, 2, 512], P('panel', None, None, 'lon'), may hold values from 0 to 8158, as said below
- lat_weights: float32 [2, 4, 2, 2, 512], P('panel', None, None, None, 'lon'), may hold values from 0 to 1, as said below
- lon_codes: int32 [2, 2, 2, 256], P('panel', None, None, 'lat'), may hold values from 0 to 8174, as said below
- lon_weights: float32 [2, 4, 2, 2, 256], P('panel', None, None, None, 'lat'), may hold values from 0 to 1, as said below
Outputs:
- pressure_out: float32 [2, 256, 512, 128], P('panel', 'lat', 'lon')
- porosity_out: float32 [2, 256, 512, 128], P('panel', 'lat', 'lon')
The draws below stay inside these ranges and needn't reach their ends.
Inputs may be any that keep to these rules, and one draw needn't show every extreme that they name: `lat_codes`: an intersection map of the shell, which may differ from draw to draw: code = a * 32 + c with a < 255 a latitude of the whole panel and c < 31 an offset inside the longitude block of the ghost cell. `lon_codes`: an intersection map of the shell, which may differ from draw to draw: code = b * 16 + r with b < 511 a longitude of the whole panel and r < 15 an offset inside the latitude block of the ghost cell. `lat_weights`: the four weights of a ghost cell are non-negative and sum to one. `lon_weights`: the four weights of a ghost cell are non-negative and sum to one.
All inputs are finite; a program needn't handle non-finite values.
Results may differ from the reference program's by a relative error of at most 0.0003.
Values sent between devices are 32-bit elements; how exact they have to be, the bound alone decides.
A program may use at most 64 MiB of HBM per device.

```python
import math
import jax
import jax.numpy as jnp

LAT_DEV = 16
LON_DEV = 32
R = 128
SWEEPS = 3
NLAT = 256
NLON = 512


def draw_source(key, part):
    values = jnp.clip(jax.random.normal(key, (2, NLAT, NLON, R), jnp.float32), -6.0, 6.0)
    return values


def intersection_map(key, count, span, block):
    phase = jax.random.randint(key, (2, 2, 2, 1), 0, count)
    along = jnp.arange(count, dtype=jnp.int32)[None, None, None, :]
    place = (along + phase) % count
    tri = jnp.minimum(place, count - place)
    half_count = count // 2
    outer = tri * (span - 2) // half_count
    outer = jnp.clip(outer, 0, span - 2)
    inner = along % block * (block - 1) // block
    inner = jnp.clip(inner, 0, block - 2)
    codes = outer * block + inner
    codes = codes.at[0, 0, 0, 0].set(0)
    codes = codes.at[1, 1, 1, count - 1].set((span - 2) * block + block - 2)
    return codes.astype(jnp.int32)


def draw_lat_codes(key, part):
    return intersection_map(jax.random.fold_in(key, 11), NLON, NLAT, LON_DEV)


def draw_lon_codes(key, part):
    return intersection_map(jax.random.fold_in(key, 23), NLAT, NLON, LAT_DEV)


def bilinear(key, count):
    first_key, second_key = jax.random.split(key)
    along_lat = jax.random.uniform(first_key, (2, 2, 2, count), jnp.float32)
    along_lon = jax.random.uniform(second_key, (2, 2, 2, count), jnp.float32)
    return jnp.stack([(1.0 - along_lat) * (1.0 - along_lon), (1.0 - along_lat) * along_lon, along_lat * (1.0 - along_lon), along_lat * along_lon], axis=1)


def draw_lat_weights(key, part):
    return bilinear(jax.random.fold_in(key, 37), NLON)


def draw_lon_weights(key, part):
    return bilinear(jax.random.fold_in(key, 41), NLAT)


def block_levels(own_key, shape, pieces, low, top_value):
    level, own = 1.0, jax.random.fold_in(own_key, 6)
    for axis_at, blocks in pieces:
        heights = jnp.exp(jax.random.uniform(jax.random.fold_in(own, axis_at), (blocks,), jnp.float32, low / len(pieces), top_value / len(pieces)))
        level = level * jnp.repeat(heights, shape[axis_at] // blocks).reshape([-1 if axis == axis_at else 1 for axis in range(len(shape))])
    return level


def bell_draw(rng, extent, scale, reach, cuts=(), held_as=jnp.bfloat16):
    drawn = jax.random.normal(rng, extent, jnp.float32) * scale
    if len(cuts) > 0:
        drawn = block_levels(rng, extent, cuts, -0.22, 0.18) * drawn
    return jnp.clip(drawn, min=-reach, max=reach).astype(held_as)


def setup_inputs(seed: int = 0) -> dict:
    arg_keys = jax.random.split(jax.random.key(seed), 9)
    return {
        "pressure": bell_draw(arg_keys[0], (2, NLAT, NLON, R), 1.0, 6.0, ((0, 2), (1, 16), (2, 16)), jnp.float32),
        "porosity": jnp.clip(0.5 + 1.5 * jax.random.uniform(arg_keys[1], (2, NLAT, NLON, R), jnp.float32) ** block_levels(arg_keys[1], (2, NLAT, NLON, R), ((0, 2), (1, 16), (2, 16)), -0.2, 0.2), 0.5, 2.0),
        "source": draw_source(jax.random.fold_in(arg_keys[8], 71), 0),
        "bulk": jnp.clip(jnp.exp(math.log(2.0) - 1.3862944 * jax.random.uniform(arg_keys[3], (2, NLAT, NLON, R), jnp.float32) ** block_levels(arg_keys[3], (2, NLAT, NLON, R), ((0, 2), (1, 16), (2, 16)), -0.2, 0.2)), 0.5, 2.0),
        "lat_codes": draw_lat_codes(jax.random.fold_in(arg_keys[8], 71), 0),
        "lat_weights": draw_lat_weights(jax.random.fold_in(arg_keys[8], 71), 0),
        "lon_codes": draw_lon_codes(jax.random.fold_in(arg_keys[8], 71), 0),
        "lon_weights": draw_lon_weights(jax.random.fold_in(arg_keys[8], 71), 0),
    }


stencil_offsets = ((0, 0), (0, 1), (1, 0), (1, 1))
radial_weight = 0.25
buoyancy = 0.5
time_step = 0.04


def pad_last(values, before, after):
    widths = [(0, 0)] * (values.ndim - 1) + [(before, after)]
    return jnp.pad(values, widths)


def lat_ghosts(source_panel, codes, weights, width):
    chosen = codes[:, :width]
    rows_at = chosen // LON_DEV
    columns = jnp.arange(NLON, dtype=jnp.int32)
    cols_at = (columns // LON_DEV) * LON_DEV + chosen % LON_DEV
    total = jnp.zeros(chosen.shape + (R,), jnp.float32)
    for corner, (row_step, col_step) in enumerate(stencil_offsets):
        picked = source_panel[rows_at + row_step, cols_at + col_step]
        total = total + weights[corner, :, :width][..., None] * picked
    return total


def lon_ghosts(source_panel, codes, weights, width):
    chosen = codes[:, :width]
    cols_at = chosen // LAT_DEV
    rows_all = jnp.arange(NLAT, dtype=jnp.int32)
    rows_at = (rows_all // LAT_DEV) * LAT_DEV + chosen % LAT_DEV
    total = jnp.zeros(chosen.shape + (R,), jnp.float32)
    for corner, (row_step, col_step) in enumerate(stencil_offsets):
        picked = source_panel[rows_at + row_step, cols_at + col_step]
        total = total + weights[corner, :, :width][..., None] * picked
    return total


def surround(field, width, lat_codes, lat_weights, lon_codes, lon_weights):
    padded = jnp.zeros((2, NLAT + 2 * width, NLON + 2 * width, R), jnp.float32)
    padded = padded.at[:, width:width + NLAT, width:width + NLON].set(field)
    for panel_dest in range(2):
        source_side = 1 - panel_dest
        north_south = lat_ghosts(field[source_side], lat_codes[source_side], lat_weights[source_side], width)
        west_east = lon_ghosts(field[source_side], lon_codes[source_side], lon_weights[source_side], width)
        padded = padded.at[panel_dest, :width, width:width + NLON].set(north_south[0][::-1])
        padded = padded.at[panel_dest, width + NLAT:, width:width + NLON].set(north_south[1])
        padded = padded.at[panel_dest, width:width + NLAT, :width].set(jnp.moveaxis(west_east[0][::-1], 0, 1))
        padded = padded.at[panel_dest, width:width + NLAT, width + NLON:].set(jnp.moveaxis(west_east[1], 0, 1))
    return padded


def face_terms(mobility):
    lat_face = 0.5 * (mobility[..., :-1, 1:-1, :] + mobility[..., 1:, 1:-1, :])
    lon_face = 0.5 * (mobility[..., 1:-1, :-1, :] + mobility[..., 1:-1, 1:, :])
    inner = mobility[..., 1:-1, 1:-1, :]
    mean_rad = 0.5 * (inner[..., :-1] + inner[..., 1:])
    return lat_face, lon_face, mean_rad


def diagonal_sum(bulk, lat_face, lon_face, mean_rad):
    rad_face = radial_weight * mean_rad
    total = bulk + lat_face[..., :-1, :, :] + lat_face[..., 1:, :, :]
    total = total + lon_face[..., :, :-1, :] + lon_face[..., :, 1:, :]
    return total + pad_last(rad_face, 1, 0) + pad_last(rad_face, 0, 1)


def neighbour_total(padded, source, lat_face, lon_face, mean_rad):
    inner = padded[..., 1:-1, 1:-1, :]
    rad_face = radial_weight * mean_rad
    total = source + lat_face[..., :-1, :, :] * padded[..., :-2, 1:-1, :]
    total = total + lat_face[..., 1:, :, :] * padded[..., 2:, 1:-1, :]
    total = total + lon_face[..., :, :-1, :] * padded[..., 1:-1, :-2, :]
    total = total + lon_face[..., :, 1:, :] * padded[..., 1:-1, 2:, :]
    total = total + pad_last(rad_face * inner[..., :-1], 1, 0) + pad_last(rad_face * inner[..., 1:], 0, 1)
    return total


def advect(pressure_pad, porosity_pad, lat_face, lon_face, mean_rad, bulk):
    pressure_in = pressure_pad[..., 1:-1, 1:-1, :]
    porosity_in = porosity_pad[..., 2:-2, 2:-2, :]
    lat_speed = -lat_face * (pressure_pad[..., 1:, 1:-1, :] - pressure_pad[..., :-1, 1:-1, :])
    lat_left = 1.5 * porosity_pad[..., 1:-2, 2:-2, :] - 0.5 * porosity_pad[..., :-3, 2:-2, :]
    lat_right = 1.5 * porosity_pad[..., 2:-1, 2:-2, :] - 0.5 * porosity_pad[..., 3:, 2:-2, :]
    lat_flux = lat_speed * jnp.where(lat_speed > 0, lat_left, lat_right)
    lon_speed = -lon_face * (pressure_pad[..., 1:-1, 1:, :] - pressure_pad[..., 1:-1, :-1, :])
    lon_left = 1.5 * porosity_pad[..., 2:-2, 1:-2, :] - 0.5 * porosity_pad[..., 2:-2, :-3, :]
    lon_right = 1.5 * porosity_pad[..., 2:-2, 2:-1, :] - 0.5 * porosity_pad[..., 2:-2, 3:, :]
    lon_flux = lon_speed * jnp.where(lon_speed > 0, lon_left, lon_right)
    rad_speed = -radial_weight * mean_rad * (pressure_in[..., 1:] - pressure_in[..., :-1]) + buoyancy * mean_rad
    rad_flux = rad_speed * jnp.where(rad_speed > 0, porosity_in[..., :-1], porosity_in[..., 1:])
    divergence = lat_flux[..., 1:, :, :] - lat_flux[..., :-1, :, :]
    divergence = divergence + lon_flux[..., :, 1:, :] - lon_flux[..., :, :-1, :]
    divergence = divergence + pad_last(rad_flux, 0, 1) - pad_last(rad_flux, 1, 0)
    return porosity_in - time_step * (divergence + bulk * pressure_in)


def reference(pressure, porosity, source, bulk, lat_codes, lat_weights, lon_codes, lon_weights):
    porosity_pad = surround(porosity, 2, lat_codes, lat_weights, lon_codes, lon_weights)
    near = porosity_pad[:, 1:-1, 1:-1, :]
    mobility = near * near * near
    lat_face, lon_face, mean_rad = face_terms(mobility)
    denominator = diagonal_sum(bulk, lat_face, lon_face, mean_rad)
    current = pressure
    for sweep_index in range(SWEEPS):
        padded = surround(current, 1, lat_codes, lat_weights, lon_codes, lon_weights)
        current = neighbour_total(padded, source, lat_face, lon_face, mean_rad) / denominator
    pressure_pad = surround(current, 1, lat_codes, lat_weights, lon_codes, lon_weights)
    porosity_new = advect(pressure_pad, porosity_pad, lat_face, lon_face, mean_rad, bulk)
    return current, porosity_new
```

```python
import jax
import jax.numpy as jnp
from jax import lax
from jax.sharding import PartitionSpec as P

SWEEPS = 3


stencil_offsets = ((0, 0), (0, 1), (1, 0), (1, 1))
radial_weight = 0.25
buoyancy = 0.5
time_step = 0.04


def padded_2(cells, sides, width):
    for axis, dim in sides:
        count = lax.axis_size(axis)
        ends = count - 1
        head = lax.slice_in_dim(cells, 0, width, axis=dim)
        tail = lax.slice_in_dim(cells, cells.shape[dim] - width, cells.shape[dim], axis=dim)
        cells = jnp.concatenate(
            [
                lax.ppermute(tail, axis, [(i, (i + 1) % count) for i in range(ends)]),
                cells,
                lax.ppermute(head, axis, [((i + 1) % count, i) for i in range(ends)]),
            ],
            axis=dim,
        )
    return cells


def swapped(block, axis, distance):
    count = lax.axis_size(axis)
    route = []
    for low in range(count):
        high = low | 1 << distance
        if high != low and high < count:
            route += [(low, high), (high, low)]
    return lax.ppermute(block, axis, route)


def pad_last(values, before, after):
    widths = [(0, 0)] * (values.ndim - 1) + [(before, after)]
    return jnp.pad(values, widths)


def rim_terms(field, lat_codes, lat_weights, lon_codes, lon_weights, width):
    rows_dev, cols_dev, levels = field.shape
    first_row = lax.axis_index("lat") * rows_dev
    first_col = lax.axis_index("lon") * cols_dev
    chosen = lat_codes[:, :width]
    rows_at = chosen // cols_dev - first_row
    cols_at = chosen % cols_dev
    lat_total = jnp.zeros(chosen.shape + (levels,), jnp.float32)
    for corner, (row_step, col_step) in enumerate(stencil_offsets):
        target = rows_at + row_step
        inside = (target >= 0) & (target < rows_dev)
        picked = field[jnp.clip(target, 0, rows_dev - 1), cols_at + col_step]
        lat_total = (
            lat_total + jnp.where(inside, lat_weights[corner, :, :width], 0.0)[..., None] * picked
        )
    chosen = lon_codes[:, :width]
    cols_at = chosen // rows_dev - first_col
    rows_at = chosen % rows_dev
    lon_total = jnp.zeros(chosen.shape + (levels,), jnp.float32)
    for corner, (row_step, col_step) in enumerate(stencil_offsets):
        target = cols_at + col_step
        inside = (target >= 0) & (target < cols_dev)
        picked = field[rows_at + row_step, jnp.clip(target, 0, cols_dev - 1)]
        lon_total = (
            lon_total + jnp.where(inside, lon_weights[corner, :, :width], 0.0)[..., None] * picked
        )
    return (lat_total, lon_total)


def surround(field, width, lat_codes, lat_weights, lon_codes, lon_weights):
    rows_dev, cols_dev, levels = field.shape
    padded = padded_2(field, (("lat", 0), ("lon", 1)), width)
    lat_terms, lon_terms = rim_terms(field, lat_codes, lat_weights, lon_codes, lon_weights, width)
    lat_summed = lax.psum(lat_terms, "lat")
    lon_summed = lax.psum(lon_terms, "lon")
    arrived = swapped(jnp.concatenate([lat_summed, lon_summed], axis=2), "panel", 0)
    lat_rim = arrived[:, :, :cols_dev]
    lon_rim = arrived[:, :, cols_dev:]
    lat_index = lax.axis_index("lat")
    lon_index = lax.axis_index("lon")
    last_lat = lax.axis_size("lat") - 1
    last_lon = lax.axis_size("lon") - 1
    north = jnp.where(lat_index == 0, lat_rim[0][::-1], padded[:width, width : width + cols_dev])
    padded = padded.at[:width, width : width + cols_dev].set(north)
    south = jnp.where(
        lat_index == last_lat, lat_rim[1], padded[width + rows_dev :, width : width + cols_dev]
    )
    padded = padded.at[width + rows_dev :, width : width + cols_dev].set(south)
    west = jnp.where(
        lon_index == 0,
        jnp.moveaxis(lon_rim[0][::-1], 0, 1),
        padded[width : width + rows_dev, :width],
    )
    padded = padded.at[width : width + rows_dev, :width].set(west)
    east = jnp.where(
        lon_index == last_lon,
        jnp.moveaxis(lon_rim[1], 0, 1),
        padded[width : width + rows_dev, width + cols_dev :],
    )
    padded = padded.at[width : width + rows_dev, width + cols_dev :].set(east)
    return padded


def face_terms(mobility):
    lat_face = 0.5 * (mobility[..., :-1, 1:-1, :] + mobility[..., 1:, 1:-1, :])
    lon_face = 0.5 * (mobility[..., 1:-1, :-1, :] + mobility[..., 1:-1, 1:, :])
    inner = mobility[..., 1:-1, 1:-1, :]
    mean_rad = 0.5 * (inner[..., :-1] + inner[..., 1:])
    return (lat_face, lon_face, mean_rad)


def diagonal_sum(bulk, lat_face, lon_face, mean_rad):
    rad_face = radial_weight * mean_rad
    total = bulk + lat_face[..., :-1, :, :] + lat_face[..., 1:, :, :]
    total = total + lon_face[..., :, :-1, :] + lon_face[..., :, 1:, :]
    return total + pad_last(rad_face, 1, 0) + pad_last(rad_face, 0, 1)


def neighbour_total(padded, source, lat_face, lon_face, mean_rad):
    inner = padded[..., 1:-1, 1:-1, :]
    rad_face = radial_weight * mean_rad
    total = source + lat_face[..., :-1, :, :] * padded[..., :-2, 1:-1, :]
    total = total + lat_face[..., 1:, :, :] * padded[..., 2:, 1:-1, :]
    total = total + lon_face[..., :, :-1, :] * padded[..., 1:-1, :-2, :]
    total = total + lon_face[..., :, 1:, :] * padded[..., 1:-1, 2:, :]
    total = (
        total
        + pad_last(rad_face * inner[..., :-1], 1, 0)
        + pad_last(rad_face * inner[..., 1:], 0, 1)
    )
    return total


def advect(pressure_pad, porosity_pad, lat_face, lon_face, mean_rad, bulk):
    pressure_in = pressure_pad[..., 1:-1, 1:-1, :]
    porosity_in = porosity_pad[..., 2:-2, 2:-2, :]
    lat_speed = -lat_face * (pressure_pad[..., 1:, 1:-1, :] - pressure_pad[..., :-1, 1:-1, :])
    lat_left = 1.5 * porosity_pad[..., 1:-2, 2:-2, :] - 0.5 * porosity_pad[..., :-3, 2:-2, :]
    lat_right = 1.5 * porosity_pad[..., 2:-1, 2:-2, :] - 0.5 * porosity_pad[..., 3:, 2:-2, :]
    lat_flux = lat_speed * jnp.where(lat_speed > 0, lat_left, lat_right)
    lon_speed = -lon_face * (pressure_pad[..., 1:-1, 1:, :] - pressure_pad[..., 1:-1, :-1, :])
    lon_left = 1.5 * porosity_pad[..., 2:-2, 1:-2, :] - 0.5 * porosity_pad[..., 2:-2, :-3, :]
    lon_right = 1.5 * porosity_pad[..., 2:-2, 2:-1, :] - 0.5 * porosity_pad[..., 2:-2, 3:, :]
    lon_flux = lon_speed * jnp.where(lon_speed > 0, lon_left, lon_right)
    rad_speed = (
        -radial_weight * mean_rad * (pressure_in[..., 1:] - pressure_in[..., :-1])
        + buoyancy * mean_rad
    )
    rad_flux = rad_speed * jnp.where(rad_speed > 0, porosity_in[..., :-1], porosity_in[..., 1:])
    divergence = lat_flux[..., 1:, :, :] - lat_flux[..., :-1, :, :]
    divergence = divergence + lon_flux[..., :, 1:, :] - lon_flux[..., :, :-1, :]
    divergence = divergence + pad_last(rad_flux, 0, 1) - pad_last(rad_flux, 1, 0)
    return porosity_in - time_step * (divergence + bulk * pressure_in)


def body(pressure, porosity, source, bulk, lat_codes, lat_weights, lon_codes, lon_weights):
    current = pressure[0]
    porosity_now = porosity[0]
    source_now = source[0]
    bulk_now = bulk[0]
    lat_code_now = lat_codes[0]
    lat_weight_now = lat_weights[0]
    lon_code_now = lon_codes[0]
    lon_weight_now = lon_weights[0]
    levels = porosity_now.shape[-1]
    both_pad = surround(
        jnp.concatenate([porosity_now, current], axis=-1),
        2,
        lat_code_now,
        lat_weight_now,
        lon_code_now,
        lon_weight_now,
    )
    porosity_pad = both_pad[..., :levels]
    first_pad = both_pad[1:-1, 1:-1, levels:]
    near = porosity_pad[1:-1, 1:-1, :]
    mobility = near * near * near
    lat_face, lon_face, mean_rad = face_terms(mobility)
    denominator = diagonal_sum(bulk_now, lat_face, lon_face, mean_rad)
    for sweep_index in range(SWEEPS):
        if sweep_index == 0:
            padded = first_pad
        else:
            padded = surround(
                current, 1, lat_code_now, lat_weight_now, lon_code_now, lon_weight_now
            )
        current = neighbour_total(padded, source_now, lat_face, lon_face, mean_rad) / denominator
    pressure_pad = surround(current, 1, lat_code_now, lat_weight_now, lon_code_now, lon_weight_now)
    porosity_new = advect(pressure_pad, porosity_pad, lat_face, lon_face, mean_rad, bulk_now)
    return (current[None], porosity_new[None])


def solution(mesh):
    placed = (
        P("panel", "lat", "lon", None),
        P("panel", "lat", "lon", None),
        P("panel", "lat", "lon", None),
        P("panel", "lat", "lon", None),
        P("panel", None, None, "lon"),
        P("panel", None, None, None, "lon"),
        P("panel", None, None, "lat"),
        P("panel", None, None, None, "lat"),
    )
    return jax.shard_map(
        body,
        mesh=mesh,
        in_specs=placed,
        out_specs=(P("panel", "lat", "lon", None), P("panel", "lat", "lon", None)),
        check_vma=False,
    )
```

```python
import functools

import jax
import jax.numpy as jnp
from jax import lax
from jax.experimental import pallas as pl
from jax.experimental.pallas import tpu as pltpu
from jax.sharding import PartitionSpec as P

SWEEPS = 3


stencil_offsets = ((0, 0), (0, 1), (1, 0), (1, 1))
radial_weight = 0.25
buoyancy = 0.5
time_step = 0.04


def padded_2(cells, sides, width):
    for axis, dim in sides:
        count = lax.axis_size(axis)
        ends = count - 1
        head = lax.slice_in_dim(cells, 0, width, axis=dim)
        tail = lax.slice_in_dim(cells, cells.shape[dim] - width, cells.shape[dim], axis=dim)
        cells = jnp.concatenate(
            [
                lax.ppermute(tail, axis, [(i, (i + 1) % count) for i in range(ends)]),
                cells,
                lax.ppermute(head, axis, [((i + 1) % count, i) for i in range(ends)]),
            ],
            axis=dim,
        )
    return cells


def swapped(block, axis, distance):
    count = lax.axis_size(axis)
    route = []
    for low in range(count):
        high = low | 1 << distance
        if high != low and high < count:
            route += [(low, high), (high, low)]
    return lax.ppermute(block, axis, route)


def pad_last(values, before, after):
    widths = [(0, 0)] * (values.ndim - 1) + [(before, after)]
    return jnp.pad(values, widths)


def rim_terms(field, lat_codes, lat_weights, lon_codes, lon_weights, width):
    rows_dev, cols_dev, levels = field.shape
    first_row = lax.axis_index("lat") * rows_dev
    first_col = lax.axis_index("lon") * cols_dev
    chosen = lat_codes[:, :width]
    rows_at = chosen // cols_dev - first_row
    cols_at = chosen % cols_dev
    lat_total = jnp.zeros(chosen.shape + (levels,), jnp.float32)
    for corner, (row_step, col_step) in enumerate(stencil_offsets):
        target = rows_at + row_step
        inside = (target >= 0) & (target < rows_dev)
        picked = field[jnp.clip(target, 0, rows_dev - 1), cols_at + col_step]
        lat_total = (
            lat_total + jnp.where(inside, lat_weights[corner, :, :width], 0.0)[..., None] * picked
        )
    chosen = lon_codes[:, :width]
    cols_at = chosen // rows_dev - first_col
    rows_at = chosen % rows_dev
    lon_total = jnp.zeros(chosen.shape + (levels,), jnp.float32)
    for corner, (row_step, col_step) in enumerate(stencil_offsets):
        target = cols_at + col_step
        inside = (target >= 0) & (target < cols_dev)
        picked = field[rows_at + row_step, jnp.clip(target, 0, cols_dev - 1)]
        lon_total = (
            lon_total + jnp.where(inside, lon_weights[corner, :, :width], 0.0)[..., None] * picked
        )
    return (lat_total, lon_total)


def exchange_kernel(
    axes, sizes, lat_part, lon_part, lat_rim, lon_rim, lat_buf, lon_buf, send_sems, recv_sems
):
    panel = lax.axis_index("panel")
    lat = lax.axis_index("lat")
    lon = lax.axis_index("lon")
    other = 1 - panel
    last_lat = sizes["lat"] - 1
    last_lon = sizes["lon"] - 1

    def device(at_lat, at_lon):
        coords = {"panel": other, "lat": at_lat, "lon": at_lon}
        return tuple(coords[name] for name in axes)

    routes = (
        (lat_part.at[0], lat_buf.at[lat], 0, device(0, lon)),
        (lat_part.at[1], lat_buf.at[lat], 0, device(last_lat, lon)),
        (lon_part.at[0], lon_buf.at[lon], 1, device(lat, 0)),
        (lon_part.at[1], lon_buf.at[lon], 1, device(lat, last_lon)),
    )
    copies = []
    for slot, (src, dst, recv, target) in enumerate(routes):
        copy = pltpu.make_async_remote_copy(
            src_ref=src,
            dst_ref=dst,
            send_sem=send_sems.at[slot],
            recv_sem=recv_sems.at[recv],
            device_id=target,
            device_id_type=pl.DeviceIdType.MESH,
        )
        copy.start()
        copies.append(copy)
    for copy in copies:
        copy.wait_send()

    lat_edge = (lat == 0) | (lat == last_lat)
    lon_edge = (lon == 0) | (lon == last_lon)

    @pl.when(lat_edge)
    def _():
        pltpu.make_async_copy(lat_buf, lat_buf, recv_sems.at[0]).wait()
        lat_rim[...] = jnp.sum(lat_buf[...], axis=0)

    @pl.when(jnp.logical_not(lat_edge))
    def _():
        lat_rim[...] = jnp.zeros_like(lat_rim)

    @pl.when(lon_edge)
    def _():
        pltpu.make_async_copy(lon_buf, lon_buf, recv_sems.at[1]).wait()
        lon_rim[...] = jnp.sum(lon_buf[...], axis=0)

    @pl.when(jnp.logical_not(lon_edge))
    def _():
        lon_rim[...] = jnp.zeros_like(lon_rim)


def exchange(lat_terms, lon_terms, axes):
    sizes = {name: lax.axis_size(name) for name in ("lat", "lon")}
    lat_shape = lat_terms.shape[1:]
    lon_shape = lon_terms.shape[1:]
    vmem = pl.BlockSpec(memory_space=pltpu.VMEM)
    moved = 4 * (lat_terms.size + lon_terms.size)
    return pl.pallas_call(
        functools.partial(exchange_kernel, axes, sizes),
        out_shape=(
            jax.ShapeDtypeStruct(lat_shape, jnp.float32),
            jax.ShapeDtypeStruct(lon_shape, jnp.float32),
        ),
        in_specs=[vmem, vmem],
        out_specs=(vmem, vmem),
        scratch_shapes=[
            pltpu.VMEM((sizes["lat"],) + lat_shape, jnp.float32),
            pltpu.VMEM((sizes["lon"],) + lon_shape, jnp.float32),
            pltpu.SemaphoreType.DMA((4,)),
            pltpu.SemaphoreType.DMA((2,)),
        ],
        compiler_params=pltpu.CompilerParams(has_side_effects=True),
        cost_estimate=pl.CostEstimate(flops=0, transcendentals=0, bytes_accessed=moved),
    )(lat_terms, lon_terms)


def surround(field, width, lat_codes, lat_weights, lon_codes, lon_weights, axes):
    rows_dev, cols_dev, levels = field.shape
    padded = padded_2(field, (("lat", 0), ("lon", 1)), width)
    lat_terms, lon_terms = rim_terms(field, lat_codes, lat_weights, lon_codes, lon_weights, width)
    lat_rim, lon_rim = exchange(lat_terms, lon_terms, axes)
    lat_index = lax.axis_index("lat")
    lon_index = lax.axis_index("lon")
    last_lat = lax.axis_size("lat") - 1
    last_lon = lax.axis_size("lon") - 1
    north = jnp.where(lat_index == 0, lat_rim[::-1], padded[:width, width : width + cols_dev])
    padded = padded.at[:width, width : width + cols_dev].set(north)
    south = jnp.where(
        lat_index == last_lat, lat_rim, padded[width + rows_dev :, width : width + cols_dev]
    )
    padded = padded.at[width + rows_dev :, width : width + cols_dev].set(south)
    west = jnp.where(
        lon_index == 0,
        jnp.moveaxis(lon_rim[::-1], 0, 1),
        padded[width : width + rows_dev, :width],
    )
    padded = padded.at[width : width + rows_dev, :width].set(west)
    east = jnp.where(
        lon_index == last_lon,
        jnp.moveaxis(lon_rim, 0, 1),
        padded[width : width + rows_dev, width + cols_dev :],
    )
    padded = padded.at[width : width + rows_dev, width + cols_dev :].set(east)
    return padded


def face_terms(mobility):
    lat_face = 0.5 * (mobility[..., :-1, 1:-1, :] + mobility[..., 1:, 1:-1, :])
    lon_face = 0.5 * (mobility[..., 1:-1, :-1, :] + mobility[..., 1:-1, 1:, :])
    inner = mobility[..., 1:-1, 1:-1, :]
    mean_rad = 0.5 * (inner[..., :-1] + inner[..., 1:])
    return (lat_face, lon_face, mean_rad)


def diagonal_sum(bulk, lat_face, lon_face, mean_rad):
    rad_face = radial_weight * mean_rad
    total = bulk + lat_face[..., :-1, :, :] + lat_face[..., 1:, :, :]
    total = total + lon_face[..., :, :-1, :] + lon_face[..., :, 1:, :]
    return total + pad_last(rad_face, 1, 0) + pad_last(rad_face, 0, 1)


def neighbour_total(padded, source, lat_face, lon_face, mean_rad):
    inner = padded[..., 1:-1, 1:-1, :]
    rad_face = radial_weight * mean_rad
    total = source + lat_face[..., :-1, :, :] * padded[..., :-2, 1:-1, :]
    total = total + lat_face[..., 1:, :, :] * padded[..., 2:, 1:-1, :]
    total = total + lon_face[..., :, :-1, :] * padded[..., 1:-1, :-2, :]
    total = total + lon_face[..., :, 1:, :] * padded[..., 1:-1, 2:, :]
    total = (
        total
        + pad_last(rad_face * inner[..., :-1], 1, 0)
        + pad_last(rad_face * inner[..., 1:], 0, 1)
    )
    return total


def advect(pressure_pad, porosity_pad, lat_face, lon_face, mean_rad, bulk):
    pressure_in = pressure_pad[..., 1:-1, 1:-1, :]
    porosity_in = porosity_pad[..., 2:-2, 2:-2, :]
    lat_speed = -lat_face * (pressure_pad[..., 1:, 1:-1, :] - pressure_pad[..., :-1, 1:-1, :])
    lat_left = 1.5 * porosity_pad[..., 1:-2, 2:-2, :] - 0.5 * porosity_pad[..., :-3, 2:-2, :]
    lat_right = 1.5 * porosity_pad[..., 2:-1, 2:-2, :] - 0.5 * porosity_pad[..., 3:, 2:-2, :]
    lat_flux = lat_speed * jnp.where(lat_speed > 0, lat_left, lat_right)
    lon_speed = -lon_face * (pressure_pad[..., 1:-1, 1:, :] - pressure_pad[..., 1:-1, :-1, :])
    lon_left = 1.5 * porosity_pad[..., 2:-2, 1:-2, :] - 0.5 * porosity_pad[..., 2:-2, :-3, :]
    lon_right = 1.5 * porosity_pad[..., 2:-2, 2:-1, :] - 0.5 * porosity_pad[..., 2:-2, 3:, :]
    lon_flux = lon_speed * jnp.where(lon_speed > 0, lon_left, lon_right)
    rad_speed = (
        -radial_weight * mean_rad * (pressure_in[..., 1:] - pressure_in[..., :-1])
        + buoyancy * mean_rad
    )
    rad_flux = rad_speed * jnp.where(rad_speed > 0, porosity_in[..., :-1], porosity_in[..., 1:])
    divergence = lat_flux[..., 1:, :, :] - lat_flux[..., :-1, :, :]
    divergence = divergence + lon_flux[..., :, 1:, :] - lon_flux[..., :, :-1, :]
    divergence = divergence + pad_last(rad_flux, 0, 1) - pad_last(rad_flux, 1, 0)
    return porosity_in - time_step * (divergence + bulk * pressure_in)


def body(axes, pressure, porosity, source, bulk, lat_codes, lat_weights, lon_codes, lon_weights):
    current = pressure[0]
    porosity_now = porosity[0]
    source_now = source[0]
    bulk_now = bulk[0]
    lat_code_now = lat_codes[0]
    lat_weight_now = lat_weights[0]
    lon_code_now = lon_codes[0]
    lon_weight_now = lon_weights[0]
    levels = porosity_now.shape[-1]
    both_pad = surround(
        jnp.concatenate([porosity_now, current], axis=-1),
        2,
        lat_code_now,
        lat_weight_now,
        lon_code_now,
        lon_weight_now,
        axes,
    )
    porosity_pad = both_pad[..., :levels]
    first_pad = both_pad[1:-1, 1:-1, levels:]
    near = porosity_pad[1:-1, 1:-1, :]
    mobility = near * near * near
    lat_face, lon_face, mean_rad = face_terms(mobility)
    denominator = diagonal_sum(bulk_now, lat_face, lon_face, mean_rad)
    for sweep_index in range(SWEEPS):
        if sweep_index == 0:
            padded = first_pad
        else:
            padded = surround(
                current, 1, lat_code_now, lat_weight_now, lon_code_now, lon_weight_now, axes
            )
        current = neighbour_total(padded, source_now, lat_face, lon_face, mean_rad) / denominator
    pressure_pad = surround(
        current, 1, lat_code_now, lat_weight_now, lon_code_now, lon_weight_now, axes
    )
    porosity_new = advect(pressure_pad, porosity_pad, lat_face, lon_face, mean_rad, bulk_now)
    return (current[None], porosity_new[None])


def solution(mesh):
    placed = (
        P("panel", "lat", "lon", None),
        P("panel", "lat", "lon", None),
        P("panel", "lat", "lon", None),
        P("panel", "lat", "lon", None),
        P("panel", None, None, "lon"),
        P("panel", None, None, None, "lon"),
        P("panel", None, None, "lat"),
        P("panel", None, None, None, "lat"),
    )
    return jax.shard_map(
        functools.partial(body, tuple(mesh.axis_names)),
        mesh=mesh,
        in_specs=placed,
        out_specs=(P("panel", "lat", "lon", None), P("panel", "lat", "lon", None)),
        check_vma=False,
    )
```

```python
import functools

import jax
import jax.numpy as jnp
from jax import lax
from jax.experimental import pallas as pl
from jax.experimental.pallas import tpu as pltpu
from jax.sharding import PartitionSpec as P

SWEEPS = 3


stencil_offsets = ((0, 0), (0, 1), (1, 0), (1, 1))
radial_weight = 0.25
buoyancy = 0.5
time_step = 0.04


def padded_2(cells, sides, width):
    for axis, dim in sides:
        count = lax.axis_size(axis)
        ends = count - 1
        head = lax.slice_in_dim(cells, 0, width, axis=dim)
        tail = lax.slice_in_dim(cells, cells.shape[dim] - width, cells.shape[dim], axis=dim)
        cells = jnp.concatenate(
            [
                lax.ppermute(tail, axis, [(i, (i + 1) % count) for i in range(ends)]),
                cells,
                lax.ppermute(head, axis, [((i + 1) % count, i) for i in range(ends)]),
            ],
            axis=dim,
        )
    return cells


def swapped(block, axis, distance):
    count = lax.axis_size(axis)
    route = []
    for low in range(count):
        high = low | 1 << distance
        if high != low and high < count:
            route += [(low, high), (high, low)]
    return lax.ppermute(block, axis, route)


def pad_last(values, before, after):
    widths = [(0, 0)] * (values.ndim - 1) + [(before, after)]
    return jnp.pad(values, widths)


def rim_terms(field, lat_codes, lat_weights, lon_codes, lon_weights, width):
    rows_dev, cols_dev, levels = field.shape
    first_row = lax.axis_index("lat") * rows_dev
    first_col = lax.axis_index("lon") * cols_dev
    chosen = lat_codes[:, :width]
    rows_at = chosen // cols_dev - first_row
    cols_at = chosen % cols_dev
    lat_total = jnp.zeros(chosen.shape + (levels,), jnp.float32)
    for corner, (row_step, col_step) in enumerate(stencil_offsets):
        target = rows_at + row_step
        inside = (target >= 0) & (target < rows_dev)
        picked = field[jnp.clip(target, 0, rows_dev - 1), cols_at + col_step]
        lat_total = (
            lat_total + jnp.where(inside, lat_weights[corner, :, :width], 0.0)[..., None] * picked
        )
    chosen = lon_codes[:, :width]
    cols_at = chosen // rows_dev - first_col
    rows_at = chosen % rows_dev
    lon_total = jnp.zeros(chosen.shape + (levels,), jnp.float32)
    for corner, (row_step, col_step) in enumerate(stencil_offsets):
        target = cols_at + col_step
        inside = (target >= 0) & (target < cols_dev)
        picked = field[rows_at + row_step, jnp.clip(target, 0, cols_dev - 1)]
        lon_total = (
            lon_total + jnp.where(inside, lon_weights[corner, :, :width], 0.0)[..., None] * picked
        )
    return (lat_total, lon_total)


def exchange_kernel(
    axes, sizes, lat_part, lon_part, lat_rim, lon_rim, lat_buf, lon_buf, send_sems, recv_sems
):
    panel = lax.axis_index("panel")
    lat = lax.axis_index("lat")
    lon = lax.axis_index("lon")
    other = 1 - panel
    last_lat = sizes["lat"] - 1
    last_lon = sizes["lon"] - 1

    def device(at_lat, at_lon):
        coords = {"panel": other, "lat": at_lat, "lon": at_lon}
        return tuple(coords[name] for name in axes)

    routes = (
        (lat_part.at[0], lat_buf.at[lat], 0, device(0, lon)),
        (lat_part.at[1], lat_buf.at[lat], 0, device(last_lat, lon)),
        (lon_part.at[0], lon_buf.at[lon], 1, device(lat, 0)),
        (lon_part.at[1], lon_buf.at[lon], 1, device(lat, last_lon)),
    )
    lat_edge = (lat == 0) | (lat == last_lat)
    lon_edge = (lon == 0) | (lon == last_lon)

    barrier = pltpu.get_barrier_semaphore()

    @pl.when(lat_edge)
    def _():
        for sender in range(sizes["lat"]):
            pl.semaphore_signal(
                barrier, inc=1, device_id=device(sender, lon), device_id_type=pl.DeviceIdType.MESH
            )

    @pl.when(lon_edge)
    def _():
        for sender in range(sizes["lon"]):
            pl.semaphore_signal(
                barrier, inc=1, device_id=device(lat, sender), device_id_type=pl.DeviceIdType.MESH
            )

    pl.semaphore_wait(barrier, len(routes))
    copies = []
    for slot, (src, dst, recv, target) in enumerate(routes):
        copy = pltpu.make_async_remote_copy(
            src_ref=src,
            dst_ref=dst,
            send_sem=send_sems.at[slot],
            recv_sem=recv_sems.at[recv],
            device_id=target,
            device_id_type=pl.DeviceIdType.MESH,
        )
        copy.start()
        copies.append(copy)
    for copy in copies:
        copy.wait_send()

    @pl.when(lat_edge)
    def _():
        pltpu.make_async_copy(lat_buf, lat_buf, recv_sems.at[0]).wait()
        lat_rim[...] = jnp.sum(lat_buf[...], axis=0)

    @pl.when(jnp.logical_not(lat_edge))
    def _():
        lat_rim[...] = jnp.zeros_like(lat_rim)

    @pl.when(lon_edge)
    def _():
        pltpu.make_async_copy(lon_buf, lon_buf, recv_sems.at[1]).wait()
        lon_rim[...] = jnp.sum(lon_buf[...], axis=0)

    @pl.when(jnp.logical_not(lon_edge))
    def _():
        lon_rim[...] = jnp.zeros_like(lon_rim)


def exchange(lat_terms, lon_terms, axes, kernel_id):
    sizes = {name: lax.axis_size(name) for name in ("lat", "lon")}
    lat_shape = lat_terms.shape[1:]
    lon_shape = lon_terms.shape[1:]
    vmem = pl.BlockSpec(memory_space=pltpu.VMEM)
    moved = 4 * (lat_terms.size + lon_terms.size)
    return pl.pallas_call(
        functools.partial(exchange_kernel, axes, sizes),
        out_shape=(
            jax.ShapeDtypeStruct(lat_shape, jnp.float32),
            jax.ShapeDtypeStruct(lon_shape, jnp.float32),
        ),
        in_specs=[vmem, vmem],
        out_specs=(vmem, vmem),
        scratch_shapes=[
            pltpu.VMEM((sizes["lat"],) + lat_shape, jnp.float32),
            pltpu.VMEM((sizes["lon"],) + lon_shape, jnp.float32),
            pltpu.SemaphoreType.DMA((4,)),
            pltpu.SemaphoreType.DMA((2,)),
        ],
        compiler_params=pltpu.CompilerParams(collective_id=kernel_id, has_side_effects=True),
        cost_estimate=pl.CostEstimate(flops=0, transcendentals=0, bytes_accessed=moved),
    )(lat_terms, lon_terms)


def surround(field, width, lat_codes, lat_weights, lon_codes, lon_weights, axes):
    rows_dev, cols_dev, levels = field.shape
    padded = padded_2(field, (("lat", 0), ("lon", 1)), width)
    lat_terms, lon_terms = rim_terms(field, lat_codes, lat_weights, lon_codes, lon_weights, width)
    lat_rim, lon_rim = exchange(lat_terms, lon_terms, axes, width - 1)
    lat_index = lax.axis_index("lat")
    lon_index = lax.axis_index("lon")
    last_lat = lax.axis_size("lat") - 1
    last_lon = lax.axis_size("lon") - 1
    north = jnp.where(lat_index == 0, lat_rim[::-1], padded[:width, width : width + cols_dev])
    padded = padded.at[:width, width : width + cols_dev].set(north)
    south = jnp.where(
        lat_index == last_lat, lat_rim, padded[width + rows_dev :, width : width + cols_dev]
    )
    padded = padded.at[width + rows_dev :, width : width + cols_dev].set(south)
    west = jnp.where(
        lon_index == 0,
        jnp.moveaxis(lon_rim[::-1], 0, 1),
        padded[width : width + rows_dev, :width],
    )
    padded = padded.at[width : width + rows_dev, :width].set(west)
    east = jnp.where(
        lon_index == last_lon,
        jnp.moveaxis(lon_rim, 0, 1),
        padded[width : width + rows_dev, width + cols_dev :],
    )
    padded = padded.at[width : width + rows_dev, width + cols_dev :].set(east)
    return padded


def face_terms(mobility):
    lat_face = 0.5 * (mobility[..., :-1, 1:-1, :] + mobility[..., 1:, 1:-1, :])
    lon_face = 0.5 * (mobility[..., 1:-1, :-1, :] + mobility[..., 1:-1, 1:, :])
    inner = mobility[..., 1:-1, 1:-1, :]
    mean_rad = 0.5 * (inner[..., :-1] + inner[..., 1:])
    return (lat_face, lon_face, mean_rad)


def diagonal_sum(bulk, lat_face, lon_face, mean_rad):
    rad_face = radial_weight * mean_rad
    total = bulk + lat_face[..., :-1, :, :] + lat_face[..., 1:, :, :]
    total = total + lon_face[..., :, :-1, :] + lon_face[..., :, 1:, :]
    return total + pad_last(rad_face, 1, 0) + pad_last(rad_face, 0, 1)


def neighbour_total(padded, source, lat_face, lon_face, mean_rad):
    inner = padded[..., 1:-1, 1:-1, :]
    rad_face = radial_weight * mean_rad
    total = source + lat_face[..., :-1, :, :] * padded[..., :-2, 1:-1, :]
    total = total + lat_face[..., 1:, :, :] * padded[..., 2:, 1:-1, :]
    total = total + lon_face[..., :, :-1, :] * padded[..., 1:-1, :-2, :]
    total = total + lon_face[..., :, 1:, :] * padded[..., 1:-1, 2:, :]
    total = (
        total
        + pad_last(rad_face * inner[..., :-1], 1, 0)
        + pad_last(rad_face * inner[..., 1:], 0, 1)
    )
    return total


def advect(pressure_pad, porosity_pad, lat_face, lon_face, mean_rad, bulk):
    pressure_in = pressure_pad[..., 1:-1, 1:-1, :]
    porosity_in = porosity_pad[..., 2:-2, 2:-2, :]
    lat_speed = -lat_face * (pressure_pad[..., 1:, 1:-1, :] - pressure_pad[..., :-1, 1:-1, :])
    lat_left = 1.5 * porosity_pad[..., 1:-2, 2:-2, :] - 0.5 * porosity_pad[..., :-3, 2:-2, :]
    lat_right = 1.5 * porosity_pad[..., 2:-1, 2:-2, :] - 0.5 * porosity_pad[..., 3:, 2:-2, :]
    lat_flux = lat_speed * jnp.where(lat_speed > 0, lat_left, lat_right)
    lon_speed = -lon_face * (pressure_pad[..., 1:-1, 1:, :] - pressure_pad[..., 1:-1, :-1, :])
    lon_left = 1.5 * porosity_pad[..., 2:-2, 1:-2, :] - 0.5 * porosity_pad[..., 2:-2, :-3, :]
    lon_right = 1.5 * porosity_pad[..., 2:-2, 2:-1, :] - 0.5 * porosity_pad[..., 2:-2, 3:, :]
    lon_flux = lon_speed * jnp.where(lon_speed > 0, lon_left, lon_right)
    rad_speed = (
        -radial_weight * mean_rad * (pressure_in[..., 1:] - pressure_in[..., :-1])
        + buoyancy * mean_rad
    )
    rad_flux = rad_speed * jnp.where(rad_speed > 0, porosity_in[..., :-1], porosity_in[..., 1:])
    divergence = lat_flux[..., 1:, :, :] - lat_flux[..., :-1, :, :]
    divergence = divergence + lon_flux[..., :, 1:, :] - lon_flux[..., :, :-1, :]
    divergence = divergence + pad_last(rad_flux, 0, 1) - pad_last(rad_flux, 1, 0)
    return porosity_in - time_step * (divergence + bulk * pressure_in)


def body(axes, pressure, porosity, source, bulk, lat_codes, lat_weights, lon_codes, lon_weights):
    current = pressure[0]
    porosity_now = porosity[0]
    source_now = source[0]
    bulk_now = bulk[0]
    lat_code_now = lat_codes[0]
    lat_weight_now = lat_weights[0]
    lon_code_now = lon_codes[0]
    lon_weight_now = lon_weights[0]
    levels = porosity_now.shape[-1]
    both_pad = surround(
        jnp.concatenate([porosity_now, current], axis=-1),
        2,
        lat_code_now,
        lat_weight_now,
        lon_code_now,
        lon_weight_now,
        axes,
    )
    porosity_pad = both_pad[..., :levels]
    first_pad = both_pad[1:-1, 1:-1, levels:]
    near = porosity_pad[1:-1, 1:-1, :]
    mobility = near * near * near
    lat_face, lon_face, mean_rad = face_terms(mobility)
    denominator = diagonal_sum(bulk_now, lat_face, lon_face, mean_rad)
    for sweep_index in range(SWEEPS):
        if sweep_index == 0:
            padded = first_pad
        else:
            padded = surround(
                current, 1, lat_code_now, lat_weight_now, lon_code_now, lon_weight_now, axes
            )
        current = neighbour_total(padded, source_now, lat_face, lon_face, mean_rad) / denominator
    pressure_pad = surround(
        current, 1, lat_code_now, lat_weight_now, lon_code_now, lon_weight_now, axes
    )
    porosity_new = advect(pressure_pad, porosity_pad, lat_face, lon_face, mean_rad, bulk_now)
    return (current[None], porosity_new[None])


def solution(mesh):
    placed = (
        P("panel", "lat", "lon", None),
        P("panel", "lat", "lon", None),
        P("panel", "lat", "lon", None),
        P("panel", "lat", "lon", None),
        P("panel", None, None, "lon"),
        P("panel", None, None, None, "lon"),
        P("panel", None, None, "lat"),
        P("panel", None, None, None, "lat"),
    )
    return jax.shard_map(
        functools.partial(body, tuple(mesh.axis_names)),
        mesh=mesh,
        in_specs=placed,
        out_specs=(P("panel", "lat", "lon", None), P("panel", "lat", "lon", None)),
        check_vma=False,
    )
```

```python
import functools

import jax
import jax.numpy as jnp
from jax import lax
from jax.experimental import pallas as pl
from jax.experimental.pallas import tpu as pltpu
from jax.sharding import PartitionSpec as P

SWEEPS = 3


stencil_offsets = ((0, 0), (0, 1), (1, 0), (1, 1))
radial_weight = 0.25
buoyancy = 0.5
time_step = 0.04


def pad_last(values, before, after):
    widths = [(0, 0)] * (values.ndim - 1) + [(before, after)]
    return jnp.pad(values, widths)


def rim_terms(field, lat_codes, lat_weights, lon_codes, lon_weights, width):
    rows_dev, cols_dev, levels = field.shape
    first_row = lax.axis_index("lat") * rows_dev
    first_col = lax.axis_index("lon") * cols_dev
    chosen = lat_codes[:, :width]
    rows_at = chosen // cols_dev - first_row
    cols_at = chosen % cols_dev
    lat_total = jnp.zeros(chosen.shape + (levels,), jnp.float32)
    for corner, (row_step, col_step) in enumerate(stencil_offsets):
        target = rows_at + row_step
        inside = (target >= 0) & (target < rows_dev)
        picked = field[jnp.clip(target, 0, rows_dev - 1), cols_at + col_step]
        lat_total = (
            lat_total + jnp.where(inside, lat_weights[corner, :, :width], 0.0)[..., None] * picked
        )
    chosen = lon_codes[:, :width]
    cols_at = chosen // rows_dev - first_col
    rows_at = chosen % rows_dev
    lon_total = jnp.zeros(chosen.shape + (levels,), jnp.float32)
    for corner, (row_step, col_step) in enumerate(stencil_offsets):
        target = cols_at + col_step
        inside = (target >= 0) & (target < cols_dev)
        picked = field[rows_at + row_step, jnp.clip(target, 0, cols_dev - 1)]
        lon_total = (
            lon_total + jnp.where(inside, lon_weights[corner, :, :width], 0.0)[..., None] * picked
        )
    return (lat_total, lon_total)


def exchange_kernel(
    axes,
    sizes,
    width,
    field,
    lat_part,
    lon_part,
    north,
    south,
    west,
    east,
    lat_buf,
    lon_buf,
    north_buf,
    south_buf,
    west_buf,
    east_buf,
    send_sems,
    recv_sems,
):
    panel = lax.axis_index("panel")
    lat = lax.axis_index("lat")
    lon = lax.axis_index("lon")
    other = 1 - panel
    last_lat = sizes["lat"] - 1
    last_lon = sizes["lon"] - 1
    rows, cols = field.shape[0], field.shape[1]
    mesh_kind = pl.DeviceIdType.MESH

    def device(at_panel, at_lat, at_lon):
        coords = {"panel": at_panel, "lat": at_lat, "lon": at_lon}
        return tuple(coords[name] for name in axes)

    always = lat >= 0
    routes = (
        (always, lat_part.at[0], lat_buf.at[lat], 0, device(other, 0, lon)),
        (always, lat_part.at[1], lat_buf.at[lat], 0, device(other, last_lat, lon)),
        (always, lon_part.at[0], lon_buf.at[lon], 1, device(other, lat, 0)),
        (always, lon_part.at[1], lon_buf.at[lon], 1, device(other, lat, last_lon)),
        (
            lat < last_lat,
            field.at[pl.ds(rows - width, width)],
            north_buf,
            2,
            device(panel, lat + 1, lon),
        ),
        (lat > 0, field.at[pl.ds(0, width)], south_buf, 3, device(panel, lat - 1, lon)),
        (
            lon < last_lon,
            field.at[:, pl.ds(cols - width, width)],
            west_buf,
            4,
            device(panel, lat, lon + 1),
        ),
        (lon > 0, field.at[:, pl.ds(0, width)], east_buf, 5, device(panel, lat, lon - 1)),
    )
    lat_edge = (lat == 0) | (lat == last_lat)
    lon_edge = (lon == 0) | (lon == last_lon)

    barrier = pltpu.get_barrier_semaphore()

    def greet(target):
        pl.semaphore_signal(barrier, inc=1, device_id=target, device_id_type=mesh_kind)

    @pl.when(lat_edge)
    def _():
        for sender in range(sizes["lat"]):
            greet(device(other, sender, lon))

    @pl.when(lon_edge)
    def _():
        for sender in range(sizes["lon"]):
            greet(device(other, lat, sender))

    neighbours = (
        (lat > 0, device(panel, lat - 1, lon)),
        (lat < last_lat, device(panel, lat + 1, lon)),
        (lon > 0, device(panel, lat, lon - 1)),
        (lon < last_lon, device(panel, lat, lon + 1)),
    )
    for present, target in neighbours:

        @pl.when(present)
        def _():
            greet(target)

    def above_zero(index, count):
        return (index + count - 1) // count

    peers = (
        4
        + above_zero(lat, sizes["lat"])
        + above_zero(last_lat - lat, sizes["lat"])
        + above_zero(lon, sizes["lon"])
        + above_zero(last_lon - lon, sizes["lon"])
    )
    pl.semaphore_wait(barrier, peers)

    copies = []
    for slot, (present, src, dst, recv, target) in enumerate(routes):
        copy = pltpu.make_async_remote_copy(
            src_ref=src,
            dst_ref=dst,
            send_sem=send_sems.at[slot],
            recv_sem=recv_sems.at[recv],
            device_id=target,
            device_id_type=mesh_kind,
        )

        @pl.when(present)
        def _():
            copy.start()

        copies.append((present, copy))
    for present, copy in copies:

        @pl.when(present)
        def _():
            copy.wait_send()

    def arrived(buf, recv):
        pltpu.make_async_copy(buf, buf, recv_sems.at[recv]).wait()

    @pl.when(lat_edge)
    def _():
        arrived(lat_buf, 0)

    @pl.when(lon_edge)
    def _():
        arrived(lon_buf, 1)

    @pl.when(lat == 0)
    def _():
        total = jnp.sum(lat_buf[...], axis=0)
        for depth in range(width):
            north[width - 1 - depth] = total[depth]

    @pl.when(lat > 0)
    def _():
        arrived(north_buf, 2)
        north[...] = north_buf[...]

    @pl.when(lat == last_lat)
    def _():
        south[...] = jnp.sum(lat_buf[...], axis=0)

    @pl.when(lat < last_lat)
    def _():
        arrived(south_buf, 3)
        south[...] = south_buf[...]

    @pl.when(lon == 0)
    def _():
        total = jnp.sum(lon_buf[...], axis=0)
        for depth in range(width):
            west[width - 1 - depth] = total[depth]

    @pl.when(lon > 0)
    def _():
        arrived(west_buf, 4)
        for depth in range(width):
            west[depth] = west_buf[:, depth, :]

    @pl.when(lon == last_lon)
    def _():
        east[...] = jnp.sum(lon_buf[...], axis=0)

    @pl.when(lon < last_lon)
    def _():
        arrived(east_buf, 5)
        for depth in range(width):
            east[depth] = east_buf[:, depth, :]


def exchange(field, lat_terms, lon_terms, axes, width):
    sizes = {name: lax.axis_size(name) for name in ("lat", "lon")}
    rows, cols, levels = field.shape
    lat_shape = (width, cols, levels)
    lon_shape = (width, rows, levels)
    vmem = pl.BlockSpec(memory_space=pltpu.VMEM)
    moved = 4 * (lat_terms.size + lon_terms.size + 2 * width * (rows + cols) * levels)
    return pl.pallas_call(
        functools.partial(exchange_kernel, axes, sizes, width),
        out_shape=(
            jax.ShapeDtypeStruct(lat_shape, jnp.float32),
            jax.ShapeDtypeStruct(lat_shape, jnp.float32),
            jax.ShapeDtypeStruct(lon_shape, jnp.float32),
            jax.ShapeDtypeStruct(lon_shape, jnp.float32),
        ),
        in_specs=[vmem, vmem, vmem],
        out_specs=(vmem, vmem, vmem, vmem),
        scratch_shapes=[
            pltpu.VMEM((sizes["lat"],) + lat_shape, jnp.float32),
            pltpu.VMEM((sizes["lon"],) + lon_shape, jnp.float32),
            pltpu.VMEM(lat_shape, jnp.float32),
            pltpu.VMEM(lat_shape, jnp.float32),
            pltpu.VMEM((rows, width, levels), jnp.float32),
            pltpu.VMEM((rows, width, levels), jnp.float32),
            pltpu.SemaphoreType.DMA((8,)),
            pltpu.SemaphoreType.DMA((6,)),
        ],
        compiler_params=pltpu.CompilerParams(collective_id=width - 1, has_side_effects=True),
        cost_estimate=pl.CostEstimate(flops=0, transcendentals=0, bytes_accessed=moved),
    )(field, lat_terms, lon_terms)


def surround(field, width, lat_codes, lat_weights, lon_codes, lon_weights, axes):
    lat_terms, lon_terms = rim_terms(field, lat_codes, lat_weights, lon_codes, lon_weights, width)
    north, south, west, east = exchange(field, lat_terms, lon_terms, axes, width)
    middle = jnp.concatenate(
        [jnp.moveaxis(west, 0, 1), field, jnp.moveaxis(east, 0, 1)], axis=1
    )
    corners = ((0, 0), (width, width), (0, 0))
    return jnp.concatenate(
        [jnp.pad(north, corners), middle, jnp.pad(south, corners)], axis=0
    )


def face_terms(mobility):
    lat_face = 0.5 * (mobility[..., :-1, 1:-1, :] + mobility[..., 1:, 1:-1, :])
    lon_face = 0.5 * (mobility[..., 1:-1, :-1, :] + mobility[..., 1:-1, 1:, :])
    inner = mobility[..., 1:-1, 1:-1, :]
    mean_rad = 0.5 * (inner[..., :-1] + inner[..., 1:])
    return (lat_face, lon_face, mean_rad)


def diagonal_sum(bulk, lat_face, lon_face, mean_rad):
    rad_face = radial_weight * mean_rad
    total = bulk + lat_face[..., :-1, :, :] + lat_face[..., 1:, :, :]
    total = total + lon_face[..., :, :-1, :] + lon_face[..., :, 1:, :]
    return total + pad_last(rad_face, 1, 0) + pad_last(rad_face, 0, 1)


def neighbour_total(padded, source, lat_face, lon_face, mean_rad):
    inner = padded[..., 1:-1, 1:-1, :]
    rad_face = radial_weight * mean_rad
    total = source + lat_face[..., :-1, :, :] * padded[..., :-2, 1:-1, :]
    total = total + lat_face[..., 1:, :, :] * padded[..., 2:, 1:-1, :]
    total = total + lon_face[..., :, :-1, :] * padded[..., 1:-1, :-2, :]
    total = total + lon_face[..., :, 1:, :] * padded[..., 1:-1, 2:, :]
    total = (
        total
        + pad_last(rad_face * inner[..., :-1], 1, 0)
        + pad_last(rad_face * inner[..., 1:], 0, 1)
    )
    return total


def advect(pressure_pad, porosity_pad, lat_face, lon_face, mean_rad, bulk):
    pressure_in = pressure_pad[..., 1:-1, 1:-1, :]
    porosity_in = porosity_pad[..., 2:-2, 2:-2, :]
    lat_speed = -lat_face * (pressure_pad[..., 1:, 1:-1, :] - pressure_pad[..., :-1, 1:-1, :])
    lat_left = 1.5 * porosity_pad[..., 1:-2, 2:-2, :] - 0.5 * porosity_pad[..., :-3, 2:-2, :]
    lat_right = 1.5 * porosity_pad[..., 2:-1, 2:-2, :] - 0.5 * porosity_pad[..., 3:, 2:-2, :]
    lat_flux = lat_speed * jnp.where(lat_speed > 0, lat_left, lat_right)
    lon_speed = -lon_face * (pressure_pad[..., 1:-1, 1:, :] - pressure_pad[..., 1:-1, :-1, :])
    lon_left = 1.5 * porosity_pad[..., 2:-2, 1:-2, :] - 0.5 * porosity_pad[..., 2:-2, :-3, :]
    lon_right = 1.5 * porosity_pad[..., 2:-2, 2:-1, :] - 0.5 * porosity_pad[..., 2:-2, 3:, :]
    lon_flux = lon_speed * jnp.where(lon_speed > 0, lon_left, lon_right)
    rad_speed = (
        -radial_weight * mean_rad * (pressure_in[..., 1:] - pressure_in[..., :-1])
        + buoyancy * mean_rad
    )
    rad_flux = rad_speed * jnp.where(rad_speed > 0, porosity_in[..., :-1], porosity_in[..., 1:])
    divergence = lat_flux[..., 1:, :, :] - lat_flux[..., :-1, :, :]
    divergence = divergence + lon_flux[..., :, 1:, :] - lon_flux[..., :, :-1, :]
    divergence = divergence + pad_last(rad_flux, 0, 1) - pad_last(rad_flux, 1, 0)
    return porosity_in - time_step * (divergence + bulk * pressure_in)


def body(axes, pressure, porosity, source, bulk, lat_codes, lat_weights, lon_codes, lon_weights):
    current = pressure[0]
    porosity_now = porosity[0]
    source_now = source[0]
    bulk_now = bulk[0]
    lat_code_now = lat_codes[0]
    lat_weight_now = lat_weights[0]
    lon_code_now = lon_codes[0]
    lon_weight_now = lon_weights[0]
    levels = porosity_now.shape[-1]
    both_pad = surround(
        jnp.concatenate([porosity_now, current], axis=-1),
        2,
        lat_code_now,
        lat_weight_now,
        lon_code_now,
        lon_weight_now,
        axes,
    )
    porosity_pad = both_pad[..., :levels]
    first_pad = both_pad[1:-1, 1:-1, levels:]
    near = porosity_pad[1:-1, 1:-1, :]
    mobility = near * near * near
    lat_face, lon_face, mean_rad = face_terms(mobility)
    denominator = diagonal_sum(bulk_now, lat_face, lon_face, mean_rad)
    for sweep_index in range(SWEEPS):
        if sweep_index == 0:
            padded = first_pad
        else:
            padded = surround(
                current, 1, lat_code_now, lat_weight_now, lon_code_now, lon_weight_now, axes
            )
        current = neighbour_total(padded, source_now, lat_face, lon_face, mean_rad) / denominator
    pressure_pad = surround(
        current, 1, lat_code_now, lat_weight_now, lon_code_now, lon_weight_now, axes
    )
    porosity_new = advect(pressure_pad, porosity_pad, lat_face, lon_face, mean_rad, bulk_now)
    return (current[None], porosity_new[None])


def solution(mesh):
    placed = (
        P("panel", "lat", "lon", None),
        P("panel", "lat", "lon", None),
        P("panel", "lat", "lon", None),
        P("panel", "lat", "lon", None),
        P("panel", None, None, "lon"),
        P("panel", None, None, None, "lon"),
        P("panel", None, None, "lat"),
        P("panel", None, None, None, "lat"),
    )
    return jax.shard_map(
        functools.partial(body, tuple(mesh.axis_names)),
        mesh=mesh,
        in_specs=placed,
        out_specs=(P("panel", "lat", "lon", None), P("panel", "lat", "lon", None)),
        check_vma=False,
    )
```

```python
import functools

import jax
import jax.numpy as jnp
from jax import lax
from jax.experimental import pallas as pl
from jax.experimental.pallas import tpu as pltpu
from jax.sharding import PartitionSpec as P

SWEEPS = 3


stencil_offsets = ((0, 0), (0, 1), (1, 0), (1, 1))
radial_weight = 0.25
buoyancy = 0.5
time_step = 0.04


def pad_last(values, before, after):
    widths = [(0, 0)] * (values.ndim - 1) + [(before, after)]
    return jnp.pad(values, widths)


def rim_plan(lat_codes, lat_weights, lon_codes, lon_weights, width, rows_dev, cols_dev):
    first_row = lax.axis_index("lat") * rows_dev
    first_col = lax.axis_index("lon") * cols_dev
    rows, cols, weights = [], [], []
    chosen = lat_codes[:, :width]
    rows_at = chosen // cols_dev - first_row
    cols_at = chosen % cols_dev
    for corner, (row_step, col_step) in enumerate(stencil_offsets):
        target = rows_at + row_step
        inside = (target >= 0) & (target < rows_dev)
        rows.append([jnp.clip(target, 0, rows_dev - 1).reshape(-1)])
        cols.append([(cols_at + col_step).reshape(-1)])
        weights.append([jnp.where(inside, lat_weights[corner, :, :width], 0.0).reshape(-1)])
    chosen = lon_codes[:, :width]
    cols_at = chosen // rows_dev - first_col
    rows_at = chosen % rows_dev
    for corner, (row_step, col_step) in enumerate(stencil_offsets):
        target = cols_at + col_step
        inside = (target >= 0) & (target < cols_dev)
        rows[corner].append((rows_at + row_step).reshape(-1))
        cols[corner].append(jnp.clip(target, 0, cols_dev - 1).reshape(-1))
        weights[corner].append(jnp.where(inside, lon_weights[corner, :, :width], 0.0).reshape(-1))
    join = lambda parts: jnp.stack([jnp.concatenate(p) for p in parts])
    return join(rows), join(cols), join(weights)


def rim_terms(field, plan, width):
    rows_dev, cols_dev, levels = field.shape
    rows, cols, weights = plan
    picked = field[rows, cols]
    total = jnp.zeros(picked.shape[1:], jnp.float32)
    for corner in range(len(stencil_offsets)):
        total = total + weights[corner][:, None] * picked[corner]
    lat_count = 2 * width * cols_dev
    lat_total = total[:lat_count].reshape(2, width, cols_dev, levels)
    lon_total = total[lat_count:].reshape(2, width, rows_dev, levels)
    return (lat_total, lon_total)


def exchange_kernel(
    axes,
    sizes,
    width,
    field,
    lat_part,
    lon_part,
    north,
    south,
    west,
    east,
    lat_buf,
    lon_buf,
    north_buf,
    south_buf,
    west_buf,
    east_buf,
    send_sems,
    recv_sems,
):
    panel = lax.axis_index("panel")
    lat = lax.axis_index("lat")
    lon = lax.axis_index("lon")
    other = 1 - panel
    last_lat = sizes["lat"] - 1
    last_lon = sizes["lon"] - 1
    rows, cols = field.shape[0], field.shape[1]
    mesh_kind = pl.DeviceIdType.MESH

    def device(at_panel, at_lat, at_lon):
        coords = {"panel": at_panel, "lat": at_lat, "lon": at_lon}
        return tuple(coords[name] for name in axes)

    always = lat >= 0
    routes = (
        (always, lat_part.at[0], lat_buf.at[lat], 0, device(other, 0, lon)),
        (always, lat_part.at[1], lat_buf.at[lat], 0, device(other, last_lat, lon)),
        (always, lon_part.at[0], lon_buf.at[lon], 1, device(other, lat, 0)),
        (always, lon_part.at[1], lon_buf.at[lon], 1, device(other, lat, last_lon)),
        (
            lat < last_lat,
            field.at[pl.ds(rows - width, width)],
            north_buf,
            2,
            device(panel, lat + 1, lon),
        ),
        (lat > 0, field.at[pl.ds(0, width)], south_buf, 3, device(panel, lat - 1, lon)),
        (
            lon < last_lon,
            field.at[:, pl.ds(cols - width, width)],
            west_buf,
            4,
            device(panel, lat, lon + 1),
        ),
        (lon > 0, field.at[:, pl.ds(0, width)], east_buf, 5, device(panel, lat, lon - 1)),
    )
    lat_edge = (lat == 0) | (lat == last_lat)
    lon_edge = (lon == 0) | (lon == last_lon)

    barrier = pltpu.get_barrier_semaphore()

    def greet(target):
        pl.semaphore_signal(barrier, inc=1, device_id=target, device_id_type=mesh_kind)

    @pl.when(lat_edge)
    def _():
        for sender in range(sizes["lat"]):
            greet(device(other, sender, lon))

    @pl.when(lon_edge)
    def _():
        for sender in range(sizes["lon"]):
            greet(device(other, lat, sender))

    neighbours = (
        (lat > 0, device(panel, lat - 1, lon)),
        (lat < last_lat, device(panel, lat + 1, lon)),
        (lon > 0, device(panel, lat, lon - 1)),
        (lon < last_lon, device(panel, lat, lon + 1)),
    )
    for present, target in neighbours:

        @pl.when(present)
        def _():
            greet(target)

    def above_zero(index, count):
        return (index + count - 1) // count

    peers = (
        4
        + above_zero(lat, sizes["lat"])
        + above_zero(last_lat - lat, sizes["lat"])
        + above_zero(lon, sizes["lon"])
        + above_zero(last_lon - lon, sizes["lon"])
    )
    pl.semaphore_wait(barrier, peers)

    copies = []
    for slot, (present, src, dst, recv, target) in enumerate(routes):
        copy = pltpu.make_async_remote_copy(
            src_ref=src,
            dst_ref=dst,
            send_sem=send_sems.at[slot],
            recv_sem=recv_sems.at[recv],
            device_id=target,
            device_id_type=mesh_kind,
        )

        @pl.when(present)
        def _():
            copy.start()

        copies.append((present, copy))
    for present, copy in copies:

        @pl.when(present)
        def _():
            copy.wait_send()

    def arrived(buf, recv):
        pltpu.make_async_copy(buf, buf, recv_sems.at[recv]).wait()

    @pl.when(lat_edge)
    def _():
        arrived(lat_buf, 0)

    @pl.when(lon_edge)
    def _():
        arrived(lon_buf, 1)

    @pl.when(lat == 0)
    def _():
        total = jnp.sum(lat_buf[...], axis=0)
        for depth in range(width):
            north[width - 1 - depth] = total[depth]

    @pl.when(lat > 0)
    def _():
        arrived(north_buf, 2)
        north[...] = north_buf[...]

    @pl.when(lat == last_lat)
    def _():
        south[...] = jnp.sum(lat_buf[...], axis=0)

    @pl.when(lat < last_lat)
    def _():
        arrived(south_buf, 3)
        south[...] = south_buf[...]

    @pl.when(lon == 0)
    def _():
        total = jnp.sum(lon_buf[...], axis=0)
        for depth in range(width):
            west[width - 1 - depth] = total[depth]

    @pl.when(lon > 0)
    def _():
        arrived(west_buf, 4)
        for depth in range(width):
            west[depth] = west_buf[:, depth, :]

    @pl.when(lon == last_lon)
    def _():
        east[...] = jnp.sum(lon_buf[...], axis=0)

    @pl.when(lon < last_lon)
    def _():
        arrived(east_buf, 5)
        for depth in range(width):
            east[depth] = east_buf[:, depth, :]


def exchange(field, lat_terms, lon_terms, axes, width):
    sizes = {name: lax.axis_size(name) for name in ("lat", "lon")}
    rows, cols, levels = field.shape
    lat_shape = (width, cols, levels)
    lon_shape = (width, rows, levels)
    vmem = pl.BlockSpec(memory_space=pltpu.VMEM)
    moved = 4 * (lat_terms.size + lon_terms.size + 2 * width * (rows + cols) * levels)
    return pl.pallas_call(
        functools.partial(exchange_kernel, axes, sizes, width),
        out_shape=(
            jax.ShapeDtypeStruct(lat_shape, jnp.float32),
            jax.ShapeDtypeStruct(lat_shape, jnp.float32),
            jax.ShapeDtypeStruct(lon_shape, jnp.float32),
            jax.ShapeDtypeStruct(lon_shape, jnp.float32),
        ),
        in_specs=[vmem, vmem, vmem],
        out_specs=(vmem, vmem, vmem, vmem),
        scratch_shapes=[
            pltpu.VMEM((sizes["lat"],) + lat_shape, jnp.float32),
            pltpu.VMEM((sizes["lon"],) + lon_shape, jnp.float32),
            pltpu.VMEM(lat_shape, jnp.float32),
            pltpu.VMEM(lat_shape, jnp.float32),
            pltpu.VMEM((rows, width, levels), jnp.float32),
            pltpu.VMEM((rows, width, levels), jnp.float32),
            pltpu.SemaphoreType.DMA((8,)),
            pltpu.SemaphoreType.DMA((6,)),
        ],
        compiler_params=pltpu.CompilerParams(collective_id=width - 1, has_side_effects=True),
        cost_estimate=pl.CostEstimate(flops=0, transcendentals=0, bytes_accessed=moved),
    )(field, lat_terms, lon_terms)


def surround(field, width, plan, axes):
    lat_terms, lon_terms = rim_terms(field, plan, width)
    north, south, west, east = exchange(field, lat_terms, lon_terms, axes, width)
    middle = jnp.concatenate(
        [jnp.moveaxis(west, 0, 1), field, jnp.moveaxis(east, 0, 1)], axis=1
    )
    corners = ((0, 0), (width, width), (0, 0))
    return jnp.concatenate(
        [jnp.pad(north, corners), middle, jnp.pad(south, corners)], axis=0
    )


def face_terms(mobility):
    lat_face = 0.5 * (mobility[..., :-1, 1:-1, :] + mobility[..., 1:, 1:-1, :])
    lon_face = 0.5 * (mobility[..., 1:-1, :-1, :] + mobility[..., 1:-1, 1:, :])
    inner = mobility[..., 1:-1, 1:-1, :]
    mean_rad = 0.5 * (inner[..., :-1] + inner[..., 1:])
    return (lat_face, lon_face, mean_rad)


def diagonal_sum(bulk, lat_face, lon_face, mean_rad):
    rad_face = radial_weight * mean_rad
    total = bulk + lat_face[..., :-1, :, :] + lat_face[..., 1:, :, :]
    total = total + lon_face[..., :, :-1, :] + lon_face[..., :, 1:, :]
    return total + pad_last(rad_face, 1, 0) + pad_last(rad_face, 0, 1)


def neighbour_total(padded, source, lat_face, lon_face, mean_rad):
    inner = padded[..., 1:-1, 1:-1, :]
    rad_face = radial_weight * mean_rad
    total = source + lat_face[..., :-1, :, :] * padded[..., :-2, 1:-1, :]
    total = total + lat_face[..., 1:, :, :] * padded[..., 2:, 1:-1, :]
    total = total + lon_face[..., :, :-1, :] * padded[..., 1:-1, :-2, :]
    total = total + lon_face[..., :, 1:, :] * padded[..., 1:-1, 2:, :]
    total = (
        total
        + pad_last(rad_face * inner[..., :-1], 1, 0)
        + pad_last(rad_face * inner[..., 1:], 0, 1)
    )
    return total


def advect(pressure_pad, porosity_pad, lat_face, lon_face, mean_rad, bulk):
    pressure_in = pressure_pad[..., 1:-1, 1:-1, :]
    porosity_in = porosity_pad[..., 2:-2, 2:-2, :]
    lat_speed = -lat_face * (pressure_pad[..., 1:, 1:-1, :] - pressure_pad[..., :-1, 1:-1, :])
    lat_left = 1.5 * porosity_pad[..., 1:-2, 2:-2, :] - 0.5 * porosity_pad[..., :-3, 2:-2, :]
    lat_right = 1.5 * porosity_pad[..., 2:-1, 2:-2, :] - 0.5 * porosity_pad[..., 3:, 2:-2, :]
    lat_flux = lat_speed * jnp.where(lat_speed > 0, lat_left, lat_right)
    lon_speed = -lon_face * (pressure_pad[..., 1:-1, 1:, :] - pressure_pad[..., 1:-1, :-1, :])
    lon_left = 1.5 * porosity_pad[..., 2:-2, 1:-2, :] - 0.5 * porosity_pad[..., 2:-2, :-3, :]
    lon_right = 1.5 * porosity_pad[..., 2:-2, 2:-1, :] - 0.5 * porosity_pad[..., 2:-2, 3:, :]
    lon_flux = lon_speed * jnp.where(lon_speed > 0, lon_left, lon_right)
    rad_speed = (
        -radial_weight * mean_rad * (pressure_in[..., 1:] - pressure_in[..., :-1])
        + buoyancy * mean_rad
    )
    rad_flux = rad_speed * jnp.where(rad_speed > 0, porosity_in[..., :-1], porosity_in[..., 1:])
    divergence = lat_flux[..., 1:, :, :] - lat_flux[..., :-1, :, :]
    divergence = divergence + lon_flux[..., :, 1:, :] - lon_flux[..., :, :-1, :]
    divergence = divergence + pad_last(rad_flux, 0, 1) - pad_last(rad_flux, 1, 0)
    return porosity_in - time_step * (divergence + bulk * pressure_in)


def body(axes, pressure, porosity, source, bulk, lat_codes, lat_weights, lon_codes, lon_weights):
    current = pressure[0]
    porosity_now = porosity[0]
    source_now = source[0]
    bulk_now = bulk[0]
    lat_code_now = lat_codes[0]
    lat_weight_now = lat_weights[0]
    lon_code_now = lon_codes[0]
    lon_weight_now = lon_weights[0]
    rows_dev, cols_dev, levels = porosity_now.shape
    plans = {
        width: rim_plan(
            lat_code_now, lat_weight_now, lon_code_now, lon_weight_now, width, rows_dev, cols_dev
        )
        for width in (1, 2)
    }
    both_pad = surround(jnp.concatenate([porosity_now, current], axis=-1), 2, plans[2], axes)
    porosity_pad = both_pad[..., :levels]
    first_pad = both_pad[1:-1, 1:-1, levels:]
    near = porosity_pad[1:-1, 1:-1, :]
    mobility = near * near * near
    lat_face, lon_face, mean_rad = face_terms(mobility)
    denominator = diagonal_sum(bulk_now, lat_face, lon_face, mean_rad)
    for sweep_index in range(SWEEPS):
        if sweep_index == 0:
            padded = first_pad
        else:
            padded = surround(current, 1, plans[1], axes)
        current = neighbour_total(padded, source_now, lat_face, lon_face, mean_rad) / denominator
    pressure_pad = surround(current, 1, plans[1], axes)
    porosity_new = advect(pressure_pad, porosity_pad, lat_face, lon_face, mean_rad, bulk_now)
    return (current[None], porosity_new[None])


def solution(mesh):
    placed = (
        P("panel", "lat", "lon", None),
        P("panel", "lat", "lon", None),
        P("panel", "lat", "lon", None),
        P("panel", "lat", "lon", None),
        P("panel", None, None, "lon"),
        P("panel", None, None, None, "lon"),
        P("panel", None, None, "lat"),
        P("panel", None, None, None, "lat"),
    )
    return jax.shard_map(
        functools.partial(body, tuple(mesh.axis_names)),
        mesh=mesh,
        in_specs=placed,
        out_specs=(P("panel", "lat", "lon", None), P("panel", "lat", "lon", None)),
        check_vma=False,
    )
```

```python
import functools

import jax
import jax.numpy as jnp
from jax import lax
from jax.experimental import pallas as pl
from jax.experimental.pallas import tpu as pltpu
from jax.sharding import PartitionSpec as P

SWEEPS = 3


stencil_offsets = ((0, 0), (0, 1), (1, 0), (1, 1))
radial_weight = 0.25
buoyancy = 0.5
time_step = 0.04


def pad_last(values, before, after):
    widths = [(0, 0)] * (values.ndim - 1) + [(before, after)]
    return jnp.pad(values, widths)


def rim_plan(lat_codes, lat_weights, lon_codes, lon_weights, width, rows_dev, cols_dev):
    first_row = lax.axis_index("lat") * rows_dev
    first_col = lax.axis_index("lon") * cols_dev
    rows, cols, weights = [], [], []
    chosen = lat_codes[:, :width]
    rows_at = chosen // cols_dev - first_row
    cols_at = chosen % cols_dev
    for corner, (row_step, col_step) in enumerate(stencil_offsets):
        target = rows_at + row_step
        inside = (target >= 0) & (target < rows_dev)
        rows.append([jnp.clip(target, 0, rows_dev - 1).reshape(-1)])
        cols.append([(cols_at + col_step).reshape(-1)])
        weights.append([jnp.where(inside, lat_weights[corner, :, :width], 0.0).reshape(-1)])
    chosen = lon_codes[:, :width]
    cols_at = chosen // rows_dev - first_col
    rows_at = chosen % rows_dev
    for corner, (row_step, col_step) in enumerate(stencil_offsets):
        target = cols_at + col_step
        inside = (target >= 0) & (target < cols_dev)
        rows[corner].append((rows_at + row_step).reshape(-1))
        cols[corner].append(jnp.clip(target, 0, cols_dev - 1).reshape(-1))
        weights[corner].append(jnp.where(inside, lon_weights[corner, :, :width], 0.0).reshape(-1))
    join = lambda parts: jnp.stack([jnp.concatenate(p) for p in parts])
    return join(rows), join(cols), join(weights)


def rim_terms(field, plan, width):
    rows_dev, cols_dev, levels = field.shape
    rows, cols, weights = plan
    picked = field[rows, cols]
    total = jnp.zeros(picked.shape[1:], jnp.float32)
    for corner in range(len(stencil_offsets)):
        total = total + weights[corner][:, None] * picked[corner]
    return total


def exchange_kernel(
    axes,
    sizes,
    width,
    field,
    rim,
    north,
    south,
    west,
    east,
    lat_buf,
    lon_buf,
    north_buf,
    south_buf,
    west_buf,
    east_buf,
    send_sems,
    recv_sems,
):
    panel = lax.axis_index("panel")
    lat = lax.axis_index("lat")
    lon = lax.axis_index("lon")
    other = 1 - panel
    last_lat = sizes["lat"] - 1
    last_lon = sizes["lon"] - 1
    rows, cols = field.shape[0], field.shape[1]
    mesh_kind = pl.DeviceIdType.MESH

    def device(at_panel, at_lat, at_lon):
        coords = {"panel": at_panel, "lat": at_lat, "lon": at_lon}
        return tuple(coords[name] for name in axes)

    always = lat >= 0
    lat_span = width * cols
    lon_span = width * rows
    lat_part = [rim.at[pl.ds(edge * lat_span, lat_span)] for edge in range(2)]
    lon_part = [rim.at[pl.ds(2 * lat_span + edge * lon_span, lon_span)] for edge in range(2)]
    routes = (
        (always, lat_part[0], lat_buf.at[lat], 0, device(other, 0, lon)),
        (always, lat_part[1], lat_buf.at[lat], 0, device(other, last_lat, lon)),
        (always, lon_part[0], lon_buf.at[lon], 1, device(other, lat, 0)),
        (always, lon_part[1], lon_buf.at[lon], 1, device(other, lat, last_lon)),
        (
            lat < last_lat,
            field.at[pl.ds(rows - width, width)],
            north_buf,
            2,
            device(panel, lat + 1, lon),
        ),
        (lat > 0, field.at[pl.ds(0, width)], south_buf, 3, device(panel, lat - 1, lon)),
        (
            lon < last_lon,
            field.at[:, pl.ds(cols - width, width)],
            west_buf,
            4,
            device(panel, lat, lon + 1),
        ),
        (lon > 0, field.at[:, pl.ds(0, width)], east_buf, 5, device(panel, lat, lon - 1)),
    )
    lat_edge = (lat == 0) | (lat == last_lat)
    lon_edge = (lon == 0) | (lon == last_lon)

    barrier = pltpu.get_barrier_semaphore()

    def greet(target):
        pl.semaphore_signal(barrier, inc=1, device_id=target, device_id_type=mesh_kind)

    @pl.when(lat_edge)
    def _():
        for sender in range(sizes["lat"]):
            greet(device(other, sender, lon))

    @pl.when(lon_edge)
    def _():
        for sender in range(sizes["lon"]):
            greet(device(other, lat, sender))

    neighbours = (
        (lat > 0, device(panel, lat - 1, lon)),
        (lat < last_lat, device(panel, lat + 1, lon)),
        (lon > 0, device(panel, lat, lon - 1)),
        (lon < last_lon, device(panel, lat, lon + 1)),
    )
    for present, target in neighbours:

        @pl.when(present)
        def _():
            greet(target)

    def above_zero(index, count):
        return (index + count - 1) // count

    peers = (
        4
        + above_zero(lat, sizes["lat"])
        + above_zero(last_lat - lat, sizes["lat"])
        + above_zero(lon, sizes["lon"])
        + above_zero(last_lon - lon, sizes["lon"])
    )
    pl.semaphore_wait(barrier, peers)

    copies = []
    for slot, (present, src, dst, recv, target) in enumerate(routes):
        copy = pltpu.make_async_remote_copy(
            src_ref=src,
            dst_ref=dst,
            send_sem=send_sems.at[slot],
            recv_sem=recv_sems.at[recv],
            device_id=target,
            device_id_type=mesh_kind,
        )

        @pl.when(present)
        def _():
            copy.start()

        copies.append((present, copy))
    for present, copy in copies:

        @pl.when(present)
        def _():
            copy.wait_send()

    def arrived(buf, recv):
        pltpu.make_async_copy(buf, buf, recv_sems.at[recv]).wait()

    @pl.when(lat_edge)
    def _():
        arrived(lat_buf, 0)

    @pl.when(lon_edge)
    def _():
        arrived(lon_buf, 1)

    @pl.when(lat == 0)
    def _():
        total = jnp.sum(lat_buf[...], axis=0)
        for depth in range(width):
            north[width - 1 - depth] = total[depth * cols : (depth + 1) * cols]

    @pl.when(lat > 0)
    def _():
        arrived(north_buf, 2)
        north[...] = north_buf[...]

    @pl.when(lat == last_lat)
    def _():
        total = jnp.sum(lat_buf[...], axis=0)
        for depth in range(width):
            south[depth] = total[depth * cols : (depth + 1) * cols]

    @pl.when(lat < last_lat)
    def _():
        arrived(south_buf, 3)
        south[...] = south_buf[...]

    @pl.when(lon == 0)
    def _():
        total = jnp.sum(lon_buf[...], axis=0)
        for depth in range(width):
            west[width - 1 - depth] = total[depth * rows : (depth + 1) * rows]

    @pl.when(lon > 0)
    def _():
        arrived(west_buf, 4)
        for depth in range(width):
            west[depth] = west_buf[:, depth, :]

    @pl.when(lon == last_lon)
    def _():
        total = jnp.sum(lon_buf[...], axis=0)
        for depth in range(width):
            east[depth] = total[depth * rows : (depth + 1) * rows]

    @pl.when(lon < last_lon)
    def _():
        arrived(east_buf, 5)
        for depth in range(width):
            east[depth] = east_buf[:, depth, :]


def exchange(field, rim, axes, width):
    sizes = {name: lax.axis_size(name) for name in ("lat", "lon")}
    rows, cols, levels = field.shape
    lat_shape = (width, cols, levels)
    lon_shape = (width, rows, levels)
    vmem = pl.BlockSpec(memory_space=pltpu.VMEM)
    moved = 4 * (rim.size + 2 * width * (rows + cols) * levels)
    return pl.pallas_call(
        functools.partial(exchange_kernel, axes, sizes, width),
        out_shape=(
            jax.ShapeDtypeStruct(lat_shape, jnp.float32),
            jax.ShapeDtypeStruct(lat_shape, jnp.float32),
            jax.ShapeDtypeStruct(lon_shape, jnp.float32),
            jax.ShapeDtypeStruct(lon_shape, jnp.float32),
        ),
        in_specs=[vmem, vmem],
        out_specs=(vmem, vmem, vmem, vmem),
        scratch_shapes=[
            pltpu.VMEM((sizes["lat"], width * cols, levels), jnp.float32),
            pltpu.VMEM((sizes["lon"], width * rows, levels), jnp.float32),
            pltpu.VMEM(lat_shape, jnp.float32),
            pltpu.VMEM(lat_shape, jnp.float32),
            pltpu.VMEM((rows, width, levels), jnp.float32),
            pltpu.VMEM((rows, width, levels), jnp.float32),
            pltpu.SemaphoreType.DMA((8,)),
            pltpu.SemaphoreType.DMA((6,)),
        ],
        compiler_params=pltpu.CompilerParams(collective_id=width - 1, has_side_effects=True),
        cost_estimate=pl.CostEstimate(flops=0, transcendentals=0, bytes_accessed=moved),
    )(field, rim)


def surround(field, width, plan, axes):
    rim = rim_terms(field, plan, width)
    north, south, west, east = exchange(field, rim, axes, width)
    middle = jnp.concatenate(
        [jnp.moveaxis(west, 0, 1), field, jnp.moveaxis(east, 0, 1)], axis=1
    )
    corners = ((0, 0), (width, width), (0, 0))
    return jnp.concatenate(
        [jnp.pad(north, corners), middle, jnp.pad(south, corners)], axis=0
    )


def face_terms(mobility):
    lat_face = 0.5 * (mobility[..., :-1, 1:-1, :] + mobility[..., 1:, 1:-1, :])
    lon_face = 0.5 * (mobility[..., 1:-1, :-1, :] + mobility[..., 1:-1, 1:, :])
    inner = mobility[..., 1:-1, 1:-1, :]
    mean_rad = 0.5 * (inner[..., :-1] + inner[..., 1:])
    return (lat_face, lon_face, mean_rad)


def diagonal_sum(bulk, lat_face, lon_face, mean_rad):
    rad_face = radial_weight * mean_rad
    total = bulk + lat_face[..., :-1, :, :] + lat_face[..., 1:, :, :]
    total = total + lon_face[..., :, :-1, :] + lon_face[..., :, 1:, :]
    return total + pad_last(rad_face, 1, 0) + pad_last(rad_face, 0, 1)


def neighbour_total(padded, source, lat_face, lon_face, mean_rad):
    inner = padded[..., 1:-1, 1:-1, :]
    rad_face = radial_weight * mean_rad
    total = source + lat_face[..., :-1, :, :] * padded[..., :-2, 1:-1, :]
    total = total + lat_face[..., 1:, :, :] * padded[..., 2:, 1:-1, :]
    total = total + lon_face[..., :, :-1, :] * padded[..., 1:-1, :-2, :]
    total = total + lon_face[..., :, 1:, :] * padded[..., 1:-1, 2:, :]
    total = (
        total
        + pad_last(rad_face * inner[..., :-1], 1, 0)
        + pad_last(rad_face * inner[..., 1:], 0, 1)
    )
    return total


def advect(pressure_pad, porosity_pad, lat_face, lon_face, mean_rad, bulk):
    pressure_in = pressure_pad[..., 1:-1, 1:-1, :]
    porosity_in = porosity_pad[..., 2:-2, 2:-2, :]
    lat_speed = -lat_face * (pressure_pad[..., 1:, 1:-1, :] - pressure_pad[..., :-1, 1:-1, :])
    lat_left = 1.5 * porosity_pad[..., 1:-2, 2:-2, :] - 0.5 * porosity_pad[..., :-3, 2:-2, :]
    lat_right = 1.5 * porosity_pad[..., 2:-1, 2:-2, :] - 0.5 * porosity_pad[..., 3:, 2:-2, :]
    lat_flux = lat_speed * jnp.where(lat_speed > 0, lat_left, lat_right)
    lon_speed = -lon_face * (pressure_pad[..., 1:-1, 1:, :] - pressure_pad[..., 1:-1, :-1, :])
    lon_left = 1.5 * porosity_pad[..., 2:-2, 1:-2, :] - 0.5 * porosity_pad[..., 2:-2, :-3, :]
    lon_right = 1.5 * porosity_pad[..., 2:-2, 2:-1, :] - 0.5 * porosity_pad[..., 2:-2, 3:, :]
    lon_flux = lon_speed * jnp.where(lon_speed > 0, lon_left, lon_right)
    rad_speed = (
        -radial_weight * mean_rad * (pressure_in[..., 1:] - pressure_in[..., :-1])
        + buoyancy * mean_rad
    )
    rad_flux = rad_speed * jnp.where(rad_speed > 0, porosity_in[..., :-1], porosity_in[..., 1:])
    divergence = lat_flux[..., 1:, :, :] - lat_flux[..., :-1, :, :]
    divergence = divergence + lon_flux[..., :, 1:, :] - lon_flux[..., :, :-1, :]
    divergence = divergence + pad_last(rad_flux, 0, 1) - pad_last(rad_flux, 1, 0)
    return porosity_in - time_step * (divergence + bulk * pressure_in)


def body(axes, pressure, porosity, source, bulk, lat_codes, lat_weights, lon_codes, lon_weights):
    current = pressure[0]
    porosity_now = porosity[0]
    source_now = source[0]
    bulk_now = bulk[0]
    lat_code_now = lat_codes[0]
    lat_weight_now = lat_weights[0]
    lon_code_now = lon_codes[0]
    lon_weight_now = lon_weights[0]
    rows_dev, cols_dev, levels = porosity_now.shape
    plans = {
        width: rim_plan(
            lat_code_now, lat_weight_now, lon_code_now, lon_weight_now, width, rows_dev, cols_dev
        )
        for width in (1, 2)
    }
    both_pad = surround(jnp.concatenate([porosity_now, current], axis=-1), 2, plans[2], axes)
    porosity_pad = both_pad[..., :levels]
    first_pad = both_pad[1:-1, 1:-1, levels:]
    near = porosity_pad[1:-1, 1:-1, :]
    mobility = near * near * near
    lat_face, lon_face, mean_rad = face_terms(mobility)
    denominator = diagonal_sum(bulk_now, lat_face, lon_face, mean_rad)
    for sweep_index in range(SWEEPS):
        if sweep_index == 0:
            padded = first_pad
        else:
            padded = surround(current, 1, plans[1], axes)
        current = neighbour_total(padded, source_now, lat_face, lon_face, mean_rad) / denominator
    pressure_pad = surround(current, 1, plans[1], axes)
    porosity_new = advect(pressure_pad, porosity_pad, lat_face, lon_face, mean_rad, bulk_now)
    return (current[None], porosity_new[None])


def solution(mesh):
    placed = (
        P("panel", "lat", "lon", None),
        P("panel", "lat", "lon", None),
        P("panel", "lat", "lon", None),
        P("panel", "lat", "lon", None),
        P("panel", None, None, "lon"),
        P("panel", None, None, None, "lon"),
        P("panel", None, None, "lat"),
        P("panel", None, None, None, "lat"),
    )
    return jax.shard_map(
        functools.partial(body, tuple(mesh.axis_names)),
        mesh=mesh,
        in_specs=placed,
        out_specs=(P("panel", "lat", "lon", None), P("panel", "lat", "lon", None)),
        check_vma=False,
    )
```

```python
import functools

import jax
import jax.numpy as jnp
from jax import lax
from jax.experimental import pallas as pl
from jax.experimental.pallas import tpu as pltpu
from jax.sharding import PartitionSpec as P

SWEEPS = 3


stencil_offsets = ((0, 0), (0, 1), (1, 0), (1, 1))
radial_weight = 0.25
buoyancy = 0.5
time_step = 0.04


def pad_last(values, before, after):
    widths = [(0, 0)] * (values.ndim - 1) + [(before, after)]
    return jnp.pad(values, widths)


def rim_plan(lat_codes, lat_weights, lon_codes, lon_weights, width, rows_dev, cols_dev):
    first_row = lax.axis_index("lat") * rows_dev
    first_col = lax.axis_index("lon") * cols_dev
    rows, cols, weights = [], [], []
    chosen = lat_codes[:, :width]
    rows_at = chosen // cols_dev - first_row
    cols_at = chosen % cols_dev
    for corner, (row_step, col_step) in enumerate(stencil_offsets):
        target = rows_at + row_step
        inside = (target >= 0) & (target < rows_dev)
        rows.append([jnp.clip(target, 0, rows_dev - 1).reshape(-1)])
        cols.append([jnp.clip(cols_at + col_step, 0, cols_dev - 1).reshape(-1)])
        weights.append([jnp.where(inside, lat_weights[corner, :, :width], 0.0).reshape(-1)])
    chosen = lon_codes[:, :width]
    cols_at = chosen // rows_dev - first_col
    rows_at = chosen % rows_dev
    for corner, (row_step, col_step) in enumerate(stencil_offsets):
        target = cols_at + col_step
        inside = (target >= 0) & (target < cols_dev)
        rows[corner].append(jnp.clip(rows_at + row_step, 0, rows_dev - 1).reshape(-1))
        cols[corner].append(jnp.clip(target, 0, cols_dev - 1).reshape(-1))
        weights[corner].append(jnp.where(inside, lon_weights[corner, :, :width], 0.0).reshape(-1))
    join = lambda parts: jnp.stack([jnp.concatenate(p) for p in parts])
    return join(rows), join(cols), join(weights)


def exchange_kernel(
    axes,
    sizes,
    width,
    field,
    rows_at,
    cols_at,
    weights_at,
    north,
    south,
    west,
    east,
    rim,
    lat_buf,
    lon_buf,
    north_buf,
    south_buf,
    west_buf,
    east_buf,
    send_sems,
    recv_sems,
):
    panel = lax.axis_index("panel")
    lat = lax.axis_index("lat")
    lon = lax.axis_index("lon")
    other = 1 - panel
    last_lat = sizes["lat"] - 1
    last_lon = sizes["lon"] - 1
    rows, cols = field.shape[0], field.shape[1]
    mesh_kind = pl.DeviceIdType.MESH

    def device(at_panel, at_lat, at_lon):
        coords = {"panel": at_panel, "lat": at_lat, "lon": at_lon}
        return tuple(coords[name] for name in axes)

    always = lat >= 0
    lat_span = width * cols
    lon_span = width * rows
    lat_part = [rim.at[pl.ds(edge * lat_span, lat_span)] for edge in range(2)]
    lon_part = [rim.at[pl.ds(2 * lat_span + edge * lon_span, lon_span)] for edge in range(2)]
    routes = (
        (always, lat_part[0], lat_buf.at[lat], 0, device(other, 0, lon)),
        (always, lat_part[1], lat_buf.at[lat], 0, device(other, last_lat, lon)),
        (always, lon_part[0], lon_buf.at[lon], 1, device(other, lat, 0)),
        (always, lon_part[1], lon_buf.at[lon], 1, device(other, lat, last_lon)),
        (
            lat < last_lat,
            field.at[pl.ds(rows - width, width)],
            north_buf,
            2,
            device(panel, lat + 1, lon),
        ),
        (lat > 0, field.at[pl.ds(0, width)], south_buf, 3, device(panel, lat - 1, lon)),
        (
            lon < last_lon,
            field.at[:, pl.ds(cols - width, width)],
            west_buf,
            4,
            device(panel, lat, lon + 1),
        ),
        (lon > 0, field.at[:, pl.ds(0, width)], east_buf, 5, device(panel, lat, lon - 1)),
    )
    lat_edge = (lat == 0) | (lat == last_lat)
    lon_edge = (lon == 0) | (lon == last_lon)

    barrier = pltpu.get_barrier_semaphore()

    def greet(target):
        pl.semaphore_signal(barrier, inc=1, device_id=target, device_id_type=mesh_kind)

    @pl.when(lat_edge)
    def _():
        for sender in range(sizes["lat"]):
            greet(device(other, sender, lon))

    @pl.when(lon_edge)
    def _():
        for sender in range(sizes["lon"]):
            greet(device(other, lat, sender))

    neighbours = (
        (lat > 0, device(panel, lat - 1, lon)),
        (lat < last_lat, device(panel, lat + 1, lon)),
        (lon > 0, device(panel, lat, lon - 1)),
        (lon < last_lon, device(panel, lat, lon + 1)),
    )
    for present, target in neighbours:

        @pl.when(present)
        def _():
            greet(target)

    def gather_row(index, carry):
        total = jnp.zeros((1, field.shape[2]), jnp.float32)
        for corner in range(len(stencil_offsets)):
            picked = field[rows_at[corner, index], pl.ds(cols_at[corner, index], 1), :]
            total = total + weights_at[corner, index] * picked
        rim[pl.ds(index, 1), :] = total
        return carry

    lax.fori_loop(0, rim.shape[0], gather_row, 0)

    def above_zero(index, count):
        return (index + count - 1) // count

    peers = (
        4
        + above_zero(lat, sizes["lat"])
        + above_zero(last_lat - lat, sizes["lat"])
        + above_zero(lon, sizes["lon"])
        + above_zero(last_lon - lon, sizes["lon"])
    )
    pl.semaphore_wait(barrier, peers)

    copies = []
    for slot, (present, src, dst, recv, target) in enumerate(routes):
        copy = pltpu.make_async_remote_copy(
            src_ref=src,
            dst_ref=dst,
            send_sem=send_sems.at[slot],
            recv_sem=recv_sems.at[recv],
            device_id=target,
            device_id_type=mesh_kind,
        )

        @pl.when(present)
        def _():
            copy.start()

        copies.append((present, copy))
    for present, copy in copies:

        @pl.when(present)
        def _():
            copy.wait_send()

    def arrived(buf, recv):
        pltpu.make_async_copy(buf, buf, recv_sems.at[recv]).wait()

    @pl.when(lat_edge)
    def _():
        arrived(lat_buf, 0)

    @pl.when(lon_edge)
    def _():
        arrived(lon_buf, 1)

    @pl.when(lat == 0)
    def _():
        total = jnp.sum(lat_buf[...], axis=0)
        for depth in range(width):
            north[width - 1 - depth] = total[depth * cols : (depth + 1) * cols]

    @pl.when(lat > 0)
    def _():
        arrived(north_buf, 2)
        north[...] = north_buf[...]

    @pl.when(lat == last_lat)
    def _():
        total = jnp.sum(lat_buf[...], axis=0)
        for depth in range(width):
            south[depth] = total[depth * cols : (depth + 1) * cols]

    @pl.when(lat < last_lat)
    def _():
        arrived(south_buf, 3)
        south[...] = south_buf[...]

    @pl.when(lon == 0)
    def _():
        total = jnp.sum(lon_buf[...], axis=0)
        for depth in range(width):
            west[width - 1 - depth] = total[depth * rows : (depth + 1) * rows]

    @pl.when(lon > 0)
    def _():
        arrived(west_buf, 4)
        for depth in range(width):
            west[depth] = west_buf[:, depth, :]

    @pl.when(lon == last_lon)
    def _():
        total = jnp.sum(lon_buf[...], axis=0)
        for depth in range(width):
            east[depth] = total[depth * rows : (depth + 1) * rows]

    @pl.when(lon < last_lon)
    def _():
        arrived(east_buf, 5)
        for depth in range(width):
            east[depth] = east_buf[:, depth, :]


def exchange(field, plan, axes, width):
    sizes = {name: lax.axis_size(name) for name in ("lat", "lon")}
    rows, cols, levels = field.shape
    lat_shape = (width, cols, levels)
    lon_shape = (width, rows, levels)
    vmem = pl.BlockSpec(memory_space=pltpu.VMEM)
    count = plan[0].shape[1]
    moved = 4 * (count * levels + 2 * width * (rows + cols) * levels)
    return pl.pallas_call(
        functools.partial(exchange_kernel, axes, sizes, width),
        out_shape=(
            jax.ShapeDtypeStruct(lat_shape, jnp.float32),
            jax.ShapeDtypeStruct(lat_shape, jnp.float32),
            jax.ShapeDtypeStruct(lon_shape, jnp.float32),
            jax.ShapeDtypeStruct(lon_shape, jnp.float32),
        ),
        in_specs=[vmem] + [pl.BlockSpec(memory_space=pltpu.SMEM)] * 3,
        out_specs=(vmem, vmem, vmem, vmem),
        scratch_shapes=[
            pltpu.VMEM((count, levels), jnp.float32),
            pltpu.VMEM((sizes["lat"], width * cols, levels), jnp.float32),
            pltpu.VMEM((sizes["lon"], width * rows, levels), jnp.float32),
            pltpu.VMEM(lat_shape, jnp.float32),
            pltpu.VMEM(lat_shape, jnp.float32),
            pltpu.VMEM((rows, width, levels), jnp.float32),
            pltpu.VMEM((rows, width, levels), jnp.float32),
            pltpu.SemaphoreType.DMA((8,)),
            pltpu.SemaphoreType.DMA((6,)),
        ],
        compiler_params=pltpu.CompilerParams(collective_id=width - 1, has_side_effects=True),
        cost_estimate=pl.CostEstimate(flops=0, transcendentals=0, bytes_accessed=moved),
    )(field, *plan)


def surround(field, width, plan, axes):
    north, south, west, east = exchange(field, plan, axes, width)
    middle = jnp.concatenate(
        [jnp.moveaxis(west, 0, 1), field, jnp.moveaxis(east, 0, 1)], axis=1
    )
    corners = ((0, 0), (width, width), (0, 0))
    return jnp.concatenate(
        [jnp.pad(north, corners), middle, jnp.pad(south, corners)], axis=0
    )


def face_terms(mobility):
    lat_face = 0.5 * (mobility[..., :-1, 1:-1, :] + mobility[..., 1:, 1:-1, :])
    lon_face = 0.5 * (mobility[..., 1:-1, :-1, :] + mobility[..., 1:-1, 1:, :])
    inner = mobility[..., 1:-1, 1:-1, :]
    mean_rad = 0.5 * (inner[..., :-1] + inner[..., 1:])
    return (lat_face, lon_face, mean_rad)


def diagonal_sum(bulk, lat_face, lon_face, mean_rad):
    rad_face = radial_weight * mean_rad
    total = bulk + lat_face[..., :-1, :, :] + lat_face[..., 1:, :, :]
    total = total + lon_face[..., :, :-1, :] + lon_face[..., :, 1:, :]
    return total + pad_last(rad_face, 1, 0) + pad_last(rad_face, 0, 1)


def neighbour_total(padded, source, lat_face, lon_face, mean_rad):
    inner = padded[..., 1:-1, 1:-1, :]
    rad_face = radial_weight * mean_rad
    total = source + lat_face[..., :-1, :, :] * padded[..., :-2, 1:-1, :]
    total = total + lat_face[..., 1:, :, :] * padded[..., 2:, 1:-1, :]
    total = total + lon_face[..., :, :-1, :] * padded[..., 1:-1, :-2, :]
    total = total + lon_face[..., :, 1:, :] * padded[..., 1:-1, 2:, :]
    total = (
        total
        + pad_last(rad_face * inner[..., :-1], 1, 0)
        + pad_last(rad_face * inner[..., 1:], 0, 1)
    )
    return total


def advect(pressure_pad, porosity_pad, lat_face, lon_face, mean_rad, bulk):
    pressure_in = pressure_pad[..., 1:-1, 1:-1, :]
    porosity_in = porosity_pad[..., 2:-2, 2:-2, :]
    lat_speed = -lat_face * (pressure_pad[..., 1:, 1:-1, :] - pressure_pad[..., :-1, 1:-1, :])
    lat_left = 1.5 * porosity_pad[..., 1:-2, 2:-2, :] - 0.5 * porosity_pad[..., :-3, 2:-2, :]
    lat_right = 1.5 * porosity_pad[..., 2:-1, 2:-2, :] - 0.5 * porosity_pad[..., 3:, 2:-2, :]
    lat_flux = lat_speed * jnp.where(lat_speed > 0, lat_left, lat_right)
    lon_speed = -lon_face * (pressure_pad[..., 1:-1, 1:, :] - pressure_pad[..., 1:-1, :-1, :])
    lon_left = 1.5 * porosity_pad[..., 2:-2, 1:-2, :] - 0.5 * porosity_pad[..., 2:-2, :-3, :]
    lon_right = 1.5 * porosity_pad[..., 2:-2, 2:-1, :] - 0.5 * porosity_pad[..., 2:-2, 3:, :]
    lon_flux = lon_speed * jnp.where(lon_speed > 0, lon_left, lon_right)
    rad_speed = (
        -radial_weight * mean_rad * (pressure_in[..., 1:] - pressure_in[..., :-1])
        + buoyancy * mean_rad
    )
    rad_flux = rad_speed * jnp.where(rad_speed > 0, porosity_in[..., :-1], porosity_in[..., 1:])
    divergence = lat_flux[..., 1:, :, :] - lat_flux[..., :-1, :, :]
    divergence = divergence + lon_flux[..., :, 1:, :] - lon_flux[..., :, :-1, :]
    divergence = divergence + pad_last(rad_flux, 0, 1) - pad_last(rad_flux, 1, 0)
    return porosity_in - time_step * (divergence + bulk * pressure_in)


def body(axes, pressure, porosity, source, bulk, lat_codes, lat_weights, lon_codes, lon_weights):
    current = pressure[0]
    porosity_now = porosity[0]
    source_now = source[0]
    bulk_now = bulk[0]
    lat_code_now = lat_codes[0]
    lat_weight_now = lat_weights[0]
    lon_code_now = lon_codes[0]
    lon_weight_now = lon_weights[0]
    rows_dev, cols_dev, levels = porosity_now.shape
    plans = {
        width: rim_plan(
            lat_code_now, lat_weight_now, lon_code_now, lon_weight_now, width, rows_dev, cols_dev
        )
        for width in (1, 2)
    }
    both_pad = surround(jnp.concatenate([porosity_now, current], axis=-1), 2, plans[2], axes)
    porosity_pad = both_pad[..., :levels]
    first_pad = both_pad[1:-1, 1:-1, levels:]
    near = porosity_pad[1:-1, 1:-1, :]
    mobility = near * near * near
    lat_face, lon_face, mean_rad = face_terms(mobility)
    denominator = diagonal_sum(bulk_now, lat_face, lon_face, mean_rad)
    for sweep_index in range(SWEEPS):
        if sweep_index == 0:
            padded = first_pad
        else:
            padded = surround(current, 1, plans[1], axes)
        current = neighbour_total(padded, source_now, lat_face, lon_face, mean_rad) / denominator
    pressure_pad = surround(current, 1, plans[1], axes)
    porosity_new = advect(pressure_pad, porosity_pad, lat_face, lon_face, mean_rad, bulk_now)
    return (current[None], porosity_new[None])


def solution(mesh):
    placed = (
        P("panel", "lat", "lon", None),
        P("panel", "lat", "lon", None),
        P("panel", "lat", "lon", None),
        P("panel", "lat", "lon", None),
        P("panel", None, None, "lon"),
        P("panel", None, None, None, "lon"),
        P("panel", None, None, "lat"),
        P("panel", None, None, None, "lat"),
    )
    return jax.shard_map(
        functools.partial(body, tuple(mesh.axis_names)),
        mesh=mesh,
        in_specs=placed,
        out_specs=(P("panel", "lat", "lon", None), P("panel", "lat", "lon", None)),
        check_vma=False,
    )
```

```python
import functools

import jax
import jax.numpy as jnp
from jax import lax
from jax.experimental import pallas as pl
from jax.experimental.pallas import tpu as pltpu
from jax.sharding import PartitionSpec as P

SWEEPS = 3


stencil_offsets = ((0, 0), (0, 1), (1, 0), (1, 1))
radial_weight = 0.25
buoyancy = 0.5
time_step = 0.04


def pad_last(values, before, after):
    widths = [(0, 0)] * (values.ndim - 1) + [(before, after)]
    return jnp.pad(values, widths)


def rim_plan(lat_codes, lat_weights, lon_codes, lon_weights, width, rows_dev, cols_dev):
    first_row = lax.axis_index("lat") * rows_dev
    first_col = lax.axis_index("lon") * cols_dev
    rows, cols, weights = [], [], []
    chosen = lat_codes[:, :width]
    rows_at = chosen // cols_dev - first_row
    cols_at = chosen % cols_dev
    for corner, (row_step, col_step) in enumerate(stencil_offsets):
        target = rows_at + row_step
        inside = (target >= 0) & (target < rows_dev)
        rows.append([jnp.clip(target, 0, rows_dev - 1).reshape(-1)])
        cols.append([jnp.clip(cols_at + col_step, 0, cols_dev - 1).reshape(-1)])
        weights.append([jnp.where(inside, lat_weights[corner, :, :width], 0.0).reshape(-1)])
    chosen = lon_codes[:, :width]
    cols_at = chosen // rows_dev - first_col
    rows_at = chosen % rows_dev
    for corner, (row_step, col_step) in enumerate(stencil_offsets):
        target = cols_at + col_step
        inside = (target >= 0) & (target < cols_dev)
        rows[corner].append(jnp.clip(rows_at + row_step, 0, rows_dev - 1).reshape(-1))
        cols[corner].append(jnp.clip(target, 0, cols_dev - 1).reshape(-1))
        weights[corner].append(jnp.where(inside, lon_weights[corner, :, :width], 0.0).reshape(-1))
    join = lambda parts: jnp.stack([jnp.concatenate(p) for p in parts])
    return join(rows), join(cols), join(weights)


def exchange_kernel(
    axes,
    sizes,
    width,
    field,
    rows_at,
    cols_at,
    weights_at,
    north,
    south,
    west,
    east,
    rim,
    lat_buf,
    lon_buf,
    north_buf,
    south_buf,
    west_buf,
    east_buf,
    send_sems,
    recv_sems,
):
    panel = lax.axis_index("panel")
    lat = lax.axis_index("lat")
    lon = lax.axis_index("lon")
    other = 1 - panel
    last_lat = sizes["lat"] - 1
    last_lon = sizes["lon"] - 1
    rows, cols = field.shape[0], field.shape[1]
    mesh_kind = pl.DeviceIdType.MESH

    def device(at_panel, at_lat, at_lon):
        coords = {"panel": at_panel, "lat": at_lat, "lon": at_lon}
        return tuple(coords[name] for name in axes)

    always = lat >= 0
    lat_span = width * cols
    lon_span = width * rows
    lat_part = [rim.at[pl.ds(edge * lat_span, lat_span)] for edge in range(2)]
    lon_part = [rim.at[pl.ds(2 * lat_span + edge * lon_span, lon_span)] for edge in range(2)]
    routes = (
        (always, lat_part[0], lat_buf.at[lat], 0, device(other, 0, lon)),
        (always, lat_part[1], lat_buf.at[lat], 0, device(other, last_lat, lon)),
        (always, lon_part[0], lon_buf.at[lon], 1, device(other, lat, 0)),
        (always, lon_part[1], lon_buf.at[lon], 1, device(other, lat, last_lon)),
        (
            lat < last_lat,
            field.at[pl.ds(rows - width, width)],
            north_buf,
            2,
            device(panel, lat + 1, lon),
        ),
        (lat > 0, field.at[pl.ds(0, width)], south_buf, 3, device(panel, lat - 1, lon)),
        (
            lon < last_lon,
            field.at[:, pl.ds(cols - width, width)],
            west_buf,
            4,
            device(panel, lat, lon + 1),
        ),
        (lon > 0, field.at[:, pl.ds(0, width)], east_buf, 5, device(panel, lat, lon - 1)),
    )
    lat_edge = (lat == 0) | (lat == last_lat)
    lon_edge = (lon == 0) | (lon == last_lon)

    barrier = pltpu.get_barrier_semaphore()

    def greet(target):
        pl.semaphore_signal(barrier, inc=1, device_id=target, device_id_type=mesh_kind)

    @pl.when(lat_edge)
    def _():
        for sender in range(sizes["lat"]):
            greet(device(other, sender, lon))

    @pl.when(lon_edge)
    def _():
        for sender in range(sizes["lon"]):
            greet(device(other, lat, sender))

    neighbours = (
        (lat > 0, device(panel, lat - 1, lon)),
        (lat < last_lat, device(panel, lat + 1, lon)),
        (lon > 0, device(panel, lat, lon - 1)),
        (lon < last_lon, device(panel, lat, lon + 1)),
    )
    for present, target in neighbours:

        @pl.when(present)
        def _():
            greet(target)

    def gather_row(index, carry):
        total = jnp.zeros((1, field.shape[2]), jnp.float32)
        for corner in range(len(stencil_offsets)):
            picked = field[rows_at[corner, index], pl.ds(cols_at[corner, index], 1), :]
            total = total + weights_at[corner, index] * picked
        rim[pl.ds(index, 1), :] = total
        return carry

    lax.fori_loop(0, rim.shape[0], gather_row, 0)

    def above_zero(index, count):
        return (index + count - 1) // count

    peers = (
        4
        + above_zero(lat, sizes["lat"])
        + above_zero(last_lat - lat, sizes["lat"])
        + above_zero(lon, sizes["lon"])
        + above_zero(last_lon - lon, sizes["lon"])
    )
    pl.semaphore_wait(barrier, peers)

    copies = []
    for slot, (present, src, dst, recv, target) in enumerate(routes):
        copy = pltpu.make_async_remote_copy(
            src_ref=src,
            dst_ref=dst,
            send_sem=send_sems.at[slot],
            recv_sem=recv_sems.at[recv],
            device_id=target,
            device_id_type=mesh_kind,
        )

        @pl.when(present)
        def _():
            copy.start()

        copies.append((present, copy))
    for present, copy in copies:

        @pl.when(present)
        def _():
            copy.wait_send()

    def arrived(buf, recv):
        pltpu.make_async_copy(buf, buf, recv_sems.at[recv]).wait()

    @pl.when(lat_edge)
    def _():
        arrived(lat_buf, 0)

    @pl.when(lon_edge)
    def _():
        arrived(lon_buf, 1)

    @pl.when(lat == 0)
    def _():
        total = jnp.sum(lat_buf[...], axis=0)
        for depth in range(width):
            north[width - 1 - depth] = total[depth * cols : (depth + 1) * cols]

    @pl.when(lat > 0)
    def _():
        arrived(north_buf, 2)
        north[...] = north_buf[...]

    @pl.when(lat == last_lat)
    def _():
        total = jnp.sum(lat_buf[...], axis=0)
        for depth in range(width):
            south[depth] = total[depth * cols : (depth + 1) * cols]

    @pl.when(lat < last_lat)
    def _():
        arrived(south_buf, 3)
        south[...] = south_buf[...]

    @pl.when(lon == 0)
    def _():
        total = jnp.sum(lon_buf[...], axis=0)
        for depth in range(width):
            west[width - 1 - depth] = total[depth * rows : (depth + 1) * rows]

    @pl.when(lon > 0)
    def _():
        arrived(west_buf, 4)
        for depth in range(width):
            west[depth] = west_buf[:, depth, :]

    @pl.when(lon == last_lon)
    def _():
        total = jnp.sum(lon_buf[...], axis=0)
        for depth in range(width):
            east[depth] = total[depth * rows : (depth + 1) * rows]

    @pl.when(lon < last_lon)
    def _():
        arrived(east_buf, 5)
        for depth in range(width):
            east[depth] = east_buf[:, depth, :]


def exchange(field, plan, axes, width):
    sizes = {name: lax.axis_size(name) for name in ("lat", "lon")}
    rows, cols, levels = field.shape
    lat_shape = (width, cols, levels)
    lon_shape = (width, rows, levels)
    vmem = pl.BlockSpec(memory_space=pltpu.VMEM)
    count = plan[0].shape[1]
    moved = 4 * (count * levels + 2 * width * (rows + cols) * levels)
    return pl.pallas_call(
        functools.partial(exchange_kernel, axes, sizes, width),
        out_shape=(
            jax.ShapeDtypeStruct(lat_shape, jnp.float32),
            jax.ShapeDtypeStruct(lat_shape, jnp.float32),
            jax.ShapeDtypeStruct(lon_shape, jnp.float32),
            jax.ShapeDtypeStruct(lon_shape, jnp.float32),
        ),
        in_specs=[vmem] + [pl.BlockSpec(memory_space=pltpu.SMEM)] * 3,
        out_specs=(vmem, vmem, vmem, vmem),
        scratch_shapes=[
            pltpu.VMEM((count, levels), jnp.float32),
            pltpu.VMEM((sizes["lat"], width * cols, levels), jnp.float32),
            pltpu.VMEM((sizes["lon"], width * rows, levels), jnp.float32),
            pltpu.VMEM(lat_shape, jnp.float32),
            pltpu.VMEM(lat_shape, jnp.float32),
            pltpu.VMEM((rows, width, levels), jnp.float32),
            pltpu.VMEM((rows, width, levels), jnp.float32),
            pltpu.SemaphoreType.DMA((8,)),
            pltpu.SemaphoreType.DMA((6,)),
        ],
        compiler_params=pltpu.CompilerParams(collective_id=width - 1, has_side_effects=True),
        cost_estimate=pl.CostEstimate(flops=0, transcendentals=0, bytes_accessed=moved),
    )(field, *plan)


def surround(field, width, plan, axes):
    north, south, west, east = exchange(field, plan, axes, width)
    middle = jnp.concatenate(
        [jnp.moveaxis(west, 0, 1), field, jnp.moveaxis(east, 0, 1)], axis=1
    )
    corners = ((0, 0), (width, width), (0, 0))
    return jnp.concatenate(
        [jnp.pad(north, corners), middle, jnp.pad(south, corners)], axis=0
    )


def face_terms(mobility):
    lat_face = 0.5 * (mobility[..., :-1, 1:-1, :] + mobility[..., 1:, 1:-1, :])
    lon_face = 0.5 * (mobility[..., 1:-1, :-1, :] + mobility[..., 1:-1, 1:, :])
    inner = mobility[..., 1:-1, 1:-1, :]
    mean_rad = 0.5 * (inner[..., :-1] + inner[..., 1:])
    return (lat_face, lon_face, mean_rad)


def diagonal_sum(bulk, lat_face, lon_face, mean_rad):
    rad_face = radial_weight * mean_rad
    total = bulk + lat_face[..., :-1, :, :] + lat_face[..., 1:, :, :]
    total = total + lon_face[..., :, :-1, :] + lon_face[..., :, 1:, :]
    return total + pad_last(rad_face, 1, 0) + pad_last(rad_face, 0, 1)


def neighbour_total(padded, source, lat_face, lon_face, mean_rad):
    inner = padded[..., 1:-1, 1:-1, :]
    rad_face = radial_weight * mean_rad
    total = source + lat_face[..., :-1, :, :] * padded[..., :-2, 1:-1, :]
    total = total + lat_face[..., 1:, :, :] * padded[..., 2:, 1:-1, :]
    total = total + lon_face[..., :, :-1, :] * padded[..., 1:-1, :-2, :]
    total = total + lon_face[..., :, 1:, :] * padded[..., 1:-1, 2:, :]
    total = (
        total
        + pad_last(rad_face * inner[..., :-1], 1, 0)
        + pad_last(rad_face * inner[..., 1:], 0, 1)
    )
    return total


def advect(pressure_pad, porosity_pad, lat_face, lon_face, mean_rad, bulk):
    pressure_in = pressure_pad[..., 1:-1, 1:-1, :]
    porosity_in = porosity_pad[..., 2:-2, 2:-2, :]
    lat_speed = -lat_face * (pressure_pad[..., 1:, 1:-1, :] - pressure_pad[..., :-1, 1:-1, :])
    lat_left = 1.5 * porosity_pad[..., 1:-2, 2:-2, :] - 0.5 * porosity_pad[..., :-3, 2:-2, :]
    lat_right = 1.5 * porosity_pad[..., 2:-1, 2:-2, :] - 0.5 * porosity_pad[..., 3:, 2:-2, :]
    lat_flux = lat_speed * jnp.where(lat_speed > 0, lat_left, lat_right)
    lon_speed = -lon_face * (pressure_pad[..., 1:-1, 1:, :] - pressure_pad[..., 1:-1, :-1, :])
    lon_left = 1.5 * porosity_pad[..., 2:-2, 1:-2, :] - 0.5 * porosity_pad[..., 2:-2, :-3, :]
    lon_right = 1.5 * porosity_pad[..., 2:-2, 2:-1, :] - 0.5 * porosity_pad[..., 2:-2, 3:, :]
    lon_flux = lon_speed * jnp.where(lon_speed > 0, lon_left, lon_right)
    rad_speed = (
        -radial_weight * mean_rad * (pressure_in[..., 1:] - pressure_in[..., :-1])
        + buoyancy * mean_rad
    )
    rad_flux = rad_speed * jnp.where(rad_speed > 0, porosity_in[..., :-1], porosity_in[..., 1:])
    divergence = lat_flux[..., 1:, :, :] - lat_flux[..., :-1, :, :]
    divergence = divergence + lon_flux[..., :, 1:, :] - lon_flux[..., :, :-1, :]
    divergence = divergence + pad_last(rad_flux, 0, 1) - pad_last(rad_flux, 1, 0)
    return porosity_in - time_step * (divergence + bulk * pressure_in)


def body(axes, pressure, porosity, source, bulk, lat_codes, lat_weights, lon_codes, lon_weights):
    current = pressure[0]
    porosity_now = porosity[0]
    source_now = source[0]
    bulk_now = bulk[0]
    lat_code_now = lat_codes[0]
    lat_weight_now = lat_weights[0]
    lon_code_now = lon_codes[0]
    lon_weight_now = lon_weights[0]
    rows_dev, cols_dev, levels = porosity_now.shape
    plans = {
        2: rim_plan(lat_code_now, lat_weight_now, lon_code_now, lon_weight_now, 2, rows_dev, cols_dev)
    }
    lat_span, lon_span = 4 * cols_dev, 2 * rows_dev
    starts = (
        (0, cols_dev),
        (2 * cols_dev, cols_dev),
        (lat_span, rows_dev),
        (lat_span + lon_span, rows_dev),
    )
    plans[1] = tuple(
        jnp.concatenate([part[:, at : at + size] for at, size in starts], axis=1)
        for part in plans[2]
    )
    both_pad = surround(jnp.concatenate([porosity_now, current], axis=-1), 2, plans[2], axes)
    porosity_pad = both_pad[..., :levels]
    first_pad = both_pad[1:-1, 1:-1, levels:]
    near = porosity_pad[1:-1, 1:-1, :]
    mobility = near * near * near
    lat_face, lon_face, mean_rad = face_terms(mobility)
    denominator = diagonal_sum(bulk_now, lat_face, lon_face, mean_rad)
    for sweep_index in range(SWEEPS):
        if sweep_index == 0:
            padded = first_pad
        else:
            padded = surround(current, 1, plans[1], axes)
        current = neighbour_total(padded, source_now, lat_face, lon_face, mean_rad) / denominator
    pressure_pad = surround(current, 1, plans[1], axes)
    porosity_new = advect(pressure_pad, porosity_pad, lat_face, lon_face, mean_rad, bulk_now)
    return (current[None], porosity_new[None])


def solution(mesh):
    placed = (
        P("panel", "lat", "lon", None),
        P("panel", "lat", "lon", None),
        P("panel", "lat", "lon", None),
        P("panel", "lat", "lon", None),
        P("panel", None, None, "lon"),
        P("panel", None, None, None, "lon"),
        P("panel", None, None, "lat"),
        P("panel", None, None, None, "lat"),
    )
    return jax.shard_map(
        functools.partial(body, tuple(mesh.axis_names)),
        mesh=mesh,
        in_specs=placed,
        out_specs=(P("panel", "lat", "lon", None), P("panel", "lat", "lon", None)),
        check_vma=False,
    )
```

```python
import functools

import jax
import jax.numpy as jnp
from jax import lax
from jax.experimental import pallas as pl
from jax.experimental.pallas import tpu as pltpu
from jax.sharding import PartitionSpec as P

SWEEPS = 3


stencil_offsets = ((0, 0), (0, 1), (1, 0), (1, 1))
radial_weight = 0.25
buoyancy = 0.5
time_step = 0.04


def pad_last(values, before, after):
    widths = [(0, 0)] * (values.ndim - 1) + [(before, after)]
    return jnp.pad(values, widths)


def rim_plan(lat_codes, lat_weights, lon_codes, lon_weights, width, rows_dev, cols_dev):
    first_row = lax.axis_index("lat") * rows_dev
    first_col = lax.axis_index("lon") * cols_dev
    rows, cols, weights = [], [], []
    chosen = lat_codes[:, :width]
    rows_at = chosen // cols_dev - first_row
    cols_at = chosen % cols_dev
    for corner, (row_step, col_step) in enumerate(stencil_offsets):
        target = rows_at + row_step
        inside = (target >= 0) & (target < rows_dev)
        rows.append([jnp.clip(target, 0, rows_dev - 1).reshape(-1)])
        cols.append([jnp.clip(cols_at + col_step, 0, cols_dev - 1).reshape(-1)])
        weights.append([jnp.where(inside, lat_weights[corner, :, :width], 0.0).reshape(-1)])
    chosen = lon_codes[:, :width]
    cols_at = chosen // rows_dev - first_col
    rows_at = chosen % rows_dev
    for corner, (row_step, col_step) in enumerate(stencil_offsets):
        target = cols_at + col_step
        inside = (target >= 0) & (target < cols_dev)
        rows[corner].append(jnp.clip(rows_at + row_step, 0, rows_dev - 1).reshape(-1))
        cols[corner].append(jnp.clip(target, 0, cols_dev - 1).reshape(-1))
        weights[corner].append(jnp.where(inside, lon_weights[corner, :, :width], 0.0).reshape(-1))
    join = lambda parts: jnp.stack([jnp.concatenate(p) for p in parts])
    return join(rows), join(cols), join(weights)


def exchange_kernel(
    axes,
    sizes,
    width,
    field,
    rows_at,
    cols_at,
    weights_at,
    north,
    south,
    west,
    east,
    rim,
    lat_buf,
    lon_buf,
    north_buf,
    south_buf,
    west_buf,
    east_buf,
    send_sems,
    recv_sems,
):
    panel = lax.axis_index("panel")
    lat = lax.axis_index("lat")
    lon = lax.axis_index("lon")
    other = 1 - panel
    last_lat = sizes["lat"] - 1
    last_lon = sizes["lon"] - 1
    rows, cols = field.shape[0], field.shape[1]
    mesh_kind = pl.DeviceIdType.MESH

    def device(at_panel, at_lat, at_lon):
        coords = {"panel": at_panel, "lat": at_lat, "lon": at_lon}
        return tuple(coords[name] for name in axes)

    always = lat >= 0
    lat_span = width * cols
    lon_span = width * rows
    lat_part = [rim.at[pl.ds(edge * lat_span, lat_span)] for edge in range(2)]
    lon_part = [rim.at[pl.ds(2 * lat_span + edge * lon_span, lon_span)] for edge in range(2)]
    routes = (
        (always, lat_part[0], lat_buf.at[lat], 0, device(other, 0, lon)),
        (always, lat_part[1], lat_buf.at[lat], 0, device(other, last_lat, lon)),
        (always, lon_part[0], lon_buf.at[lon], 1, device(other, lat, 0)),
        (always, lon_part[1], lon_buf.at[lon], 1, device(other, lat, last_lon)),
        (
            lat < last_lat,
            field.at[pl.ds(rows - width, width)],
            north_buf,
            2,
            device(panel, lat + 1, lon),
        ),
        (lat > 0, field.at[pl.ds(0, width)], south_buf, 3, device(panel, lat - 1, lon)),
        (
            lon < last_lon,
            field.at[:, pl.ds(cols - width, width)],
            west_buf,
            4,
            device(panel, lat, lon + 1),
        ),
        (lon > 0, field.at[:, pl.ds(0, width)], east_buf, 5, device(panel, lat, lon - 1)),
    )
    lat_edge = (lat == 0) | (lat == last_lat)
    lon_edge = (lon == 0) | (lon == last_lon)

    barrier = pltpu.get_barrier_semaphore()

    def greet(target):
        pl.semaphore_signal(barrier, inc=1, device_id=target, device_id_type=mesh_kind)

    @pl.when(lat_edge)
    def _():
        for sender in range(sizes["lat"]):
            greet(device(other, sender, lon))

    @pl.when(lon_edge)
    def _():
        for sender in range(sizes["lon"]):
            greet(device(other, lat, sender))

    neighbours = (
        (lat > 0, device(panel, lat - 1, lon)),
        (lat < last_lat, device(panel, lat + 1, lon)),
        (lon > 0, device(panel, lat, lon - 1)),
        (lon < last_lon, device(panel, lat, lon + 1)),
    )
    for present, target in neighbours:

        @pl.when(present)
        def _():
            greet(target)

    def gather_row(index, carry):
        total = jnp.zeros((1, field.shape[2]), jnp.float32)
        for corner in range(len(stencil_offsets)):
            picked = field[rows_at[corner, index], pl.ds(cols_at[corner, index], 1), :]
            total = total + weights_at[corner, index] * picked
        rim[pl.ds(index, 1), :] = total
        return carry

    lax.fori_loop(0, rim.shape[0], gather_row, 0)

    def above_zero(index, count):
        return (index + count - 1) // count

    peers = (
        4
        + above_zero(lat, sizes["lat"])
        + above_zero(last_lat - lat, sizes["lat"])
        + above_zero(lon, sizes["lon"])
        + above_zero(last_lon - lon, sizes["lon"])
    )
    pl.semaphore_wait(barrier, peers)

    copies = []
    for slot, (present, src, dst, recv, target) in enumerate(routes):
        copy = pltpu.make_async_remote_copy(
            src_ref=src,
            dst_ref=dst,
            send_sem=send_sems.at[slot],
            recv_sem=recv_sems.at[recv],
            device_id=target,
            device_id_type=mesh_kind,
        )

        @pl.when(present)
        def _():
            copy.start()

        copies.append((present, copy))
    for present, copy in copies:

        @pl.when(present)
        def _():
            copy.wait_send()

    corner = jnp.zeros((width, width, field.shape[2]), jnp.float32)
    for strip in (north, south):
        strip[:, pl.ds(0, width)] = corner
        strip[:, pl.ds(cols + width, width)] = corner

    def arrived(buf, recv):
        pltpu.make_async_copy(buf, buf, recv_sems.at[recv]).wait()

    @pl.when(lat_edge)
    def _():
        arrived(lat_buf, 0)

    @pl.when(lon_edge)
    def _():
        arrived(lon_buf, 1)

    @pl.when(lat == 0)
    def _():
        total = jnp.sum(lat_buf[...], axis=0)
        for depth in range(width):
            north[width - 1 - depth, pl.ds(width, cols)] = total[depth * cols : (depth + 1) * cols]

    @pl.when(lat > 0)
    def _():
        arrived(north_buf, 2)
        north[:, pl.ds(width, cols)] = north_buf[...]

    @pl.when(lat == last_lat)
    def _():
        total = jnp.sum(lat_buf[...], axis=0)
        for depth in range(width):
            south[depth, pl.ds(width, cols)] = total[depth * cols : (depth + 1) * cols]

    @pl.when(lat < last_lat)
    def _():
        arrived(south_buf, 3)
        south[:, pl.ds(width, cols)] = south_buf[...]

    @pl.when(lon == 0)
    def _():
        total = jnp.sum(lon_buf[...], axis=0)
        for depth in range(width):
            west[width - 1 - depth] = total[depth * rows : (depth + 1) * rows]

    @pl.when(lon > 0)
    def _():
        arrived(west_buf, 4)
        for depth in range(width):
            west[depth] = west_buf[:, depth, :]

    @pl.when(lon == last_lon)
    def _():
        total = jnp.sum(lon_buf[...], axis=0)
        for depth in range(width):
            east[depth] = total[depth * rows : (depth + 1) * rows]

    @pl.when(lon < last_lon)
    def _():
        arrived(east_buf, 5)
        for depth in range(width):
            east[depth] = east_buf[:, depth, :]


def exchange(field, plan, axes, width):
    sizes = {name: lax.axis_size(name) for name in ("lat", "lon")}
    rows, cols, levels = field.shape
    lat_shape = (width, cols + 2 * width, levels)
    lon_shape = (width, rows, levels)
    vmem = pl.BlockSpec(memory_space=pltpu.VMEM)
    count = plan[0].shape[1]
    moved = 4 * (count * levels + 2 * width * (rows + cols) * levels)
    return pl.pallas_call(
        functools.partial(exchange_kernel, axes, sizes, width),
        out_shape=(
            jax.ShapeDtypeStruct(lat_shape, jnp.float32),
            jax.ShapeDtypeStruct(lat_shape, jnp.float32),
            jax.ShapeDtypeStruct(lon_shape, jnp.float32),
            jax.ShapeDtypeStruct(lon_shape, jnp.float32),
        ),
        in_specs=[vmem] + [pl.BlockSpec(memory_space=pltpu.SMEM)] * 3,
        out_specs=(vmem, vmem, vmem, vmem),
        scratch_shapes=[
            pltpu.VMEM((count, levels), jnp.float32),
            pltpu.VMEM((sizes["lat"], width * cols, levels), jnp.float32),
            pltpu.VMEM((sizes["lon"], width * rows, levels), jnp.float32),
            pltpu.VMEM((width, cols, levels), jnp.float32),
            pltpu.VMEM((width, cols, levels), jnp.float32),
            pltpu.VMEM((rows, width, levels), jnp.float32),
            pltpu.VMEM((rows, width, levels), jnp.float32),
            pltpu.SemaphoreType.DMA((8,)),
            pltpu.SemaphoreType.DMA((6,)),
        ],
        compiler_params=pltpu.CompilerParams(collective_id=width - 1, has_side_effects=True),
        cost_estimate=pl.CostEstimate(flops=0, transcendentals=0, bytes_accessed=moved),
    )(field, *plan)


def surround(field, width, plan, axes):
    north, south, west, east = exchange(field, plan, axes, width)
    middle = jnp.concatenate(
        [jnp.moveaxis(west, 0, 1), field, jnp.moveaxis(east, 0, 1)], axis=1
    )
    return jnp.concatenate([north, middle, south], axis=0)


def face_terms(mobility):
    lat_face = 0.5 * (mobility[..., :-1, 1:-1, :] + mobility[..., 1:, 1:-1, :])
    lon_face = 0.5 * (mobility[..., 1:-1, :-1, :] + mobility[..., 1:-1, 1:, :])
    inner = mobility[..., 1:-1, 1:-1, :]
    mean_rad = 0.5 * (inner[..., :-1] + inner[..., 1:])
    return (lat_face, lon_face, mean_rad)


def diagonal_sum(bulk, lat_face, lon_face, mean_rad):
    rad_face = radial_weight * mean_rad
    total = bulk + lat_face[..., :-1, :, :] + lat_face[..., 1:, :, :]
    total = total + lon_face[..., :, :-1, :] + lon_face[..., :, 1:, :]
    return total + pad_last(rad_face, 1, 0) + pad_last(rad_face, 0, 1)


def neighbour_total(padded, source, lat_face, lon_face, mean_rad):
    inner = padded[..., 1:-1, 1:-1, :]
    rad_face = radial_weight * mean_rad
    total = source + lat_face[..., :-1, :, :] * padded[..., :-2, 1:-1, :]
    total = total + lat_face[..., 1:, :, :] * padded[..., 2:, 1:-1, :]
    total = total + lon_face[..., :, :-1, :] * padded[..., 1:-1, :-2, :]
    total = total + lon_face[..., :, 1:, :] * padded[..., 1:-1, 2:, :]
    total = (
        total
        + pad_last(rad_face * inner[..., :-1], 1, 0)
        + pad_last(rad_face * inner[..., 1:], 0, 1)
    )
    return total


def advect(pressure_pad, porosity_pad, lat_face, lon_face, mean_rad, bulk):
    pressure_in = pressure_pad[..., 1:-1, 1:-1, :]
    porosity_in = porosity_pad[..., 2:-2, 2:-2, :]
    lat_speed = -lat_face * (pressure_pad[..., 1:, 1:-1, :] - pressure_pad[..., :-1, 1:-1, :])
    lat_left = 1.5 * porosity_pad[..., 1:-2, 2:-2, :] - 0.5 * porosity_pad[..., :-3, 2:-2, :]
    lat_right = 1.5 * porosity_pad[..., 2:-1, 2:-2, :] - 0.5 * porosity_pad[..., 3:, 2:-2, :]
    lat_flux = lat_speed * jnp.where(lat_speed > 0, lat_left, lat_right)
    lon_speed = -lon_face * (pressure_pad[..., 1:-1, 1:, :] - pressure_pad[..., 1:-1, :-1, :])
    lon_left = 1.5 * porosity_pad[..., 2:-2, 1:-2, :] - 0.5 * porosity_pad[..., 2:-2, :-3, :]
    lon_right = 1.5 * porosity_pad[..., 2:-2, 2:-1, :] - 0.5 * porosity_pad[..., 2:-2, 3:, :]
    lon_flux = lon_speed * jnp.where(lon_speed > 0, lon_left, lon_right)
    rad_speed = (
        -radial_weight * mean_rad * (pressure_in[..., 1:] - pressure_in[..., :-1])
        + buoyancy * mean_rad
    )
    rad_flux = rad_speed * jnp.where(rad_speed > 0, porosity_in[..., :-1], porosity_in[..., 1:])
    divergence = lat_flux[..., 1:, :, :] - lat_flux[..., :-1, :, :]
    divergence = divergence + lon_flux[..., :, 1:, :] - lon_flux[..., :, :-1, :]
    divergence = divergence + pad_last(rad_flux, 0, 1) - pad_last(rad_flux, 1, 0)
    return porosity_in - time_step * (divergence + bulk * pressure_in)


def body(axes, pressure, porosity, source, bulk, lat_codes, lat_weights, lon_codes, lon_weights):
    current = pressure[0]
    porosity_now = porosity[0]
    source_now = source[0]
    bulk_now = bulk[0]
    lat_code_now = lat_codes[0]
    lat_weight_now = lat_weights[0]
    lon_code_now = lon_codes[0]
    lon_weight_now = lon_weights[0]
    rows_dev, cols_dev, levels = porosity_now.shape
    plans = {
        2: rim_plan(lat_code_now, lat_weight_now, lon_code_now, lon_weight_now, 2, rows_dev, cols_dev)
    }
    lat_span, lon_span = 4 * cols_dev, 2 * rows_dev
    starts = (
        (0, cols_dev),
        (2 * cols_dev, cols_dev),
        (lat_span, rows_dev),
        (lat_span + lon_span, rows_dev),
    )
    plans[1] = tuple(
        jnp.concatenate([part[:, at : at + size] for at, size in starts], axis=1)
        for part in plans[2]
    )
    both_pad = surround(jnp.concatenate([porosity_now, current], axis=-1), 2, plans[2], axes)
    porosity_pad = both_pad[..., :levels]
    first_pad = both_pad[1:-1, 1:-1, levels:]
    near = porosity_pad[1:-1, 1:-1, :]
    mobility = near * near * near
    lat_face, lon_face, mean_rad = face_terms(mobility)
    denominator = diagonal_sum(bulk_now, lat_face, lon_face, mean_rad)
    for sweep_index in range(SWEEPS):
        if sweep_index == 0:
            padded = first_pad
        else:
            padded = surround(current, 1, plans[1], axes)
        current = neighbour_total(padded, source_now, lat_face, lon_face, mean_rad) / denominator
    pressure_pad = surround(current, 1, plans[1], axes)
    porosity_new = advect(pressure_pad, porosity_pad, lat_face, lon_face, mean_rad, bulk_now)
    return (current[None], porosity_new[None])


def solution(mesh):
    placed = (
        P("panel", "lat", "lon", None),
        P("panel", "lat", "lon", None),
        P("panel", "lat", "lon", None),
        P("panel", "lat", "lon", None),
        P("panel", None, None, "lon"),
        P("panel", None, None, None, "lon"),
        P("panel", None, None, "lat"),
        P("panel", None, None, None, "lat"),
    )
    return jax.shard_map(
        functools.partial(body, tuple(mesh.axis_names)),
        mesh=mesh,
        in_specs=placed,
        out_specs=(P("panel", "lat", "lon", None), P("panel", "lat", "lon", None)),
        check_vma=False,
    )
```
